32 devices in a mesh: rad: 8 (over z, y), mode: 4 (over x, core).
Axes of the slice: x: 2, y: 2, z: 4, core: 2. Of those that a mesh axis runs over, the one named last changes fastest.
Arguments:
- coefficients: bfloat16 [3, 2, 256, 8, 4, 1152], P(None, None, 'rad', None, 'mode'), may hold values from -6 to 6
- legendre: bfloat16 [8, 4, 1152, 2048], P('rad', 'mode'), may hold values from -0.25 to 0.25
- radial_left_factor: float32 [3, 256, 256], replicated, may hold values from -0.375 to 0.375
- radial_right: float32 [3, 256, 256], replicated, may hold values from -0.375 to 0.375
- eigen_rates: float32 [3, 256], replicated, may hold values from 0.02 to 4
- diffusivity: float32 [3], replicated, may hold values from 0.5 to 4
- slot_order: int32 [8, 4, 2], P('rad', 'mode'), may hold values from 0 to 1023, as said below
- slot_start: int32 [8, 4, 2], P('rad', 'mode'), may hold values from 0 to 1024, as said below
Outputs:
- physical: bfloat16 [3, 2, 8, 4, 256, 2, 2048], P(None, None, None, None, 'rad', None, 'mode')
The draws below stay inside these ranges and needn't reach their ends.
Inputs may be any that keep to these rules, and one draw needn't show every extreme that they name: `slot_order`: the 64 orders are distinct, 0 and 1023 among them; the two rows of every group have block counts 1024 / 128 - floor(m / 128) that add up to exactly 9. `slot_start`: in every group the first row starts at slot 0 and the second at 128 times the first row's block count.
All inputs are finite; a program needn't handle non-finite values.
Results may differ from the reference program's by a relative error of at most 0.0049.
Values may be sent and summed in bfloat16 or wider, within the bound.
A program may use at most 256 MiB of HBM per device.

```python
import math
import jax
import jax.numpy as jnp
from jax import lax

DEGREES = 1024
BLOCK = 128
RADII = 256
LATS = 2048
RAD_COUNT = 8
MODE_COUNT = 4
PACKED = 1152
ROWS = 64
STRIDE = 16


def dealt_table(key):
    offset_key = jax.random.fold_in(key, 11)
    pairing_key = jax.random.fold_in(key, 12)
    flip_key = jax.random.fold_in(key, 13)
    position = jnp.arange(ROWS, dtype=jnp.int32)
    offsets = jax.random.randint(offset_key, (ROWS,), 0, STRIDE, dtype=jnp.int32)
    offsets = jnp.where(position == 0, 0, offsets)
    offsets = jnp.where(position == ROWS - 1, STRIDE - 1, offsets)
    orders_all = STRIDE * position + offsets
    pairing = jax.random.permutation(pairing_key, ROWS // 2).astype(jnp.int32)
    reversed_order = jax.random.randint(flip_key, (ROWS // 2,), 0, 2, dtype=jnp.int32)
    reversed_order = jnp.where(pairing == 0, 0, reversed_order)
    lower_order = orders_all[pairing]
    upper_order = orders_all[ROWS - 1 - pairing]
    leading = jnp.where(reversed_order == 1, upper_order, lower_order)
    trailing = jnp.where(reversed_order == 1, lower_order, upper_order)
    lead_start = jnp.zeros_like(leading)
    trail_start = DEGREES - BLOCK * (leading // BLOCK)
    orders = jnp.stack([leading, trailing], axis=-1).reshape(RAD_COUNT, MODE_COUNT, 2)
    begin_offsets = jnp.stack([lead_start, trail_start], axis=-1).reshape(RAD_COUNT, MODE_COUNT, 2)
    return (orders.astype(jnp.int32), begin_offsets.astype(jnp.int32))


def draw_slot_order(key, part):
    orders, begin_offsets = dealt_table(jax.random.fold_in(key, 5))
    return orders


def draw_slot_start(key, part):
    orders, begin_offsets = dealt_table(jax.random.fold_in(key, 5))
    return begin_offsets


def level_of(stream_key, extent, shards, smallest, high):
    factor_of = 1.0
    for dim, blocks in shards:
        steps = jax.random.uniform(jax.random.fold_in(jax.random.fold_in(stream_key, 6), dim), (blocks,), jnp.float32, smallest / len(shards), high / len(shards))
        factor_of = factor_of * jnp.repeat(jnp.exp(steps), extent[dim] // blocks).reshape((-1,) + (1,) * (len(extent) - 1 - dim))
    return factor_of


def gaussian(stream_key, extent, scale, most, cuts=(), kind=jnp.bfloat16):
    result = scale * jax.random.normal(stream_key, extent, jnp.float32)
    if cuts:
        result = result * level_of(stream_key, extent, cuts, -0.22, 0.18)
    return jnp.clip(result, -most, most).astype(kind)


def setup_inputs(seed: int = 0) -> dict:
    streams_of = jax.random.split(jax.random.key(seed), 9)
    coefficients = gaussian(streams_of[0], (3, 2, RADII, RAD_COUNT, MODE_COUNT, PACKED), 1.0, 6.0, ((2, 8), (4, 4)))
    legendre = gaussian(streams_of[1], (RAD_COUNT, MODE_COUNT, PACKED, LATS), (DEGREES // 2) ** -0.5, 0.25, ((0, 8), (1, 4)))
    radial_left_factor = gaussian(streams_of[2], (3, RADII, RADII), RADII ** -0.5, 0.375, (), jnp.float32)
    radial_right = gaussian(streams_of[3], (3, RADII, RADII), RADII ** -0.5, 0.375, (), jnp.float32)
    eigen_rates = jnp.clip(jnp.exp(jax.random.uniform(streams_of[4], (3, RADII), jnp.float32, math.log(0.02), math.log(4.0))), 0.02, 4.0)
    diffusivity = jnp.clip(jnp.exp(jax.random.uniform(streams_of[5], (3,), jnp.float32, math.log(0.5), math.log(4.0))), 0.5, 4.0)
    slot_order = draw_slot_order(jax.random.fold_in(streams_of[8], 71), 0)
    slot_start = draw_slot_start(jax.random.fold_in(streams_of[8], 71), 0)
    return dict(coefficients=coefficients, legendre=legendre, radial_left_factor=radial_left_factor, radial_right=radial_right, eigen_rates=eigen_rates, diffusivity=diffusivity, slot_order=slot_order, slot_start=slot_start)


def slot_layout(orders, begin_offsets):
    position = jnp.arange(PACKED, dtype=jnp.int32)
    first_degree = (BLOCK * (orders // BLOCK)).astype(jnp.int32)
    row_length = DEGREES - first_degree
    inside = (position[None, :] >= begin_offsets[:, None]) & (position[None, :] < begin_offsets[:, None] + row_length[:, None])
    degree_rows = first_degree[:, None] + position[None, :] - begin_offsets[:, None]
    active_mask = inside & (degree_rows >= orders[:, None])
    degree = jnp.sum(jnp.where(inside, degree_rows, 0), axis=0).astype(jnp.int32)
    return active_mask, degree


def one_group(pieces, radial_left_factor, radial_right, eigen_rates, diffusivity):
    spectral, polynomial_rows, orders, begin_offsets = pieces
    active_mask, degree = slot_layout(orders, begin_offsets)
    degree_level = degree.astype(jnp.float32)
    harmonic = degree_level * (degree_level + 1.0) / (DEGREES * DEGREES)
    shrink = 1.0 + eigen_rates[:, :, None] + diffusivity[:, None, None] * harmonic[None, None, :]
    covered = jnp.any(active_mask, axis=0).astype(jnp.float32)
    factor = covered[None, None, :] / shrink
    field_values = spectral.astype(jnp.float32)
    rotated_view = jnp.einsum("okg,omgx->omkx", radial_left_factor, field_values, precision=lax.Precision.HIGHEST)
    scaled = rotated_view * factor[:, None]
    updated = jnp.einsum("fts,fcsp->fctp", radial_right, scaled, precision=lax.Precision.HIGHEST).astype(jnp.bfloat16)
    per_slot = []
    for slot_index in range(2):
        masked = updated * active_mask[slot_index].astype(jnp.bfloat16)
        summed = jnp.dot(masked.reshape(6 * RADII, PACKED), polynomial_rows, preferred_element_type=jnp.float32)
        per_slot.append(summed.reshape(3, 2, RADII, LATS).astype(jnp.bfloat16))
    return jnp.stack(per_slot, axis=3)


def reference(coefficients, legendre, radial_left_factor, radial_right, eigen_rates, diffusivity, slot_order, slot_start):
    total_group_count = RAD_COUNT * MODE_COUNT
    spectral_groups = jnp.transpose(coefficients, (3, 4, 0, 1, 2, 5)).reshape(total_group_count, 3, 2, RADII, PACKED)
    legendre_groups = legendre.reshape(total_group_count, PACKED, LATS)
    order_groups = slot_order.reshape(total_group_count, 2).astype(jnp.int32)
    start_groups = slot_start.reshape(total_group_count, 2).astype(jnp.int32)
    results = lax.map(lambda pieces: one_group(pieces, radial_left_factor, radial_right, eigen_rates, diffusivity), (spectral_groups, legendre_groups, order_groups, start_groups))
    results = results.reshape(RAD_COUNT, MODE_COUNT, 3, 2, RADII, 2, LATS)
    return jnp.transpose(results, (2, 3, 0, 1, 4, 5, 6))
```

```python
import functools
import jax
import jax.numpy as jnp
from jax import lax
from jax.experimental import pallas as pl
from jax.experimental.pallas import tpu as pltpu
from jax.sharding import PartitionSpec as P

DEGREES = 1024
BLOCK = 128
MESH = pl.DeviceIdType.MESH


def far_first(count):
    return sorted(range(count), key=lambda k: (-min(k, count - k), k))


def whole_kernel(
    rads,
    modes,
    parts_count,
    order_ref,
    start_ref,
    diffusivity_ref,
    eigen_ref,
    left_hbm,
    right_hbm,
    x_ref,
    legendre_ref,
    o_ref,
    left_ref,
    right_ref,
    entering,
    outgoing,
    arrived,
    polynomial_rows,
    updated,
    held,
    enter_sem,
    in_send,
    in_recv,
    factor_sem,
    legendre_sem,
    out_send,
    out_recv,
    out_local,
):
    my_rad = lax.axis_index("rad")
    my_mode = lax.axis_index("mode")
    devices = rads * modes
    parts = arrived.shape[0]
    packed = arrived.shape[3]
    radii = right_ref.shape[1]
    rows, lats = held.shape[1], held.shape[3]
    me = my_rad * modes + my_mode

    def enter(c):
        return pltpu.make_async_copy(x_ref.at[c], entering.at[c], enter_sem.at[c])

    for c in range(parts):
        enter(c).start()
    fetches = (
        pltpu.make_async_copy(left_hbm, left_ref, factor_sem.at[0]),
        pltpu.make_async_copy(right_hbm, right_ref, factor_sem.at[1]),
        pltpu.make_async_copy(legendre_ref, polynomial_rows, legendre_sem),
    )
    for fetch in fetches:
        fetch.start()
    barrier = pltpu.get_barrier_semaphore()
    for ka in range(rads):
        for kb in range(modes):
            if ka or kb:
                peer = (lax.rem(my_rad + ka, rads), lax.rem(my_mode + kb, modes))
                pl.semaphore_signal(barrier, inc=1, device_id=peer, device_id_type=MESH)

    def turn(c):
        enter(c).wait()
        outgoing[c] = jnp.swapaxes(entering[c], 0, 1)

    turn(0)
    pl.semaphore_wait(barrier, devices - 1)

    def send_part(c, carry):
        @pl.when(c > 0)
        def _():
            turn(c)

        for ka in far_first(rads):
            a = lax.rem(my_rad + ka, rads)
            source = outgoing.at[c, a]
            target = arrived.at[c, my_rad]
            if ka:
                pltpu.make_async_remote_copy(
                    src_ref=source,
                    dst_ref=target,
                    send_sem=in_send,
                    recv_sem=in_recv.at[c],
                    device_id=(a, my_mode),
                    device_id_type=MESH,
                ).start()
            else:
                pltpu.make_async_copy(source, target, in_recv.at[c]).start()
        return carry

    lax.fori_loop(0, parts, send_part, 0)

    position = lax.broadcasted_iota(jnp.int32, (1, packed), 1)
    live = []
    degree = jnp.zeros((1, packed), jnp.int32)
    for s in range(2):
        order = order_ref[0, 0, s]
        start = start_ref[0, 0, s]
        first_degree = BLOCK * (order // BLOCK)
        inside = (position >= start) & (position < start + DEGREES - first_degree)
        row_degree = first_degree + position - start
        degree = degree + jnp.where(inside, row_degree, 0)
        live.append(jnp.where(inside & (row_degree >= order), 1.0, 0.0).astype(jnp.float32))
    degree_level = degree.astype(jnp.float32)
    harmonic = degree_level * (degree_level + 1.0) / (DEGREES * DEGREES)
    covered = jnp.maximum(live[0], live[1])
    row = lax.broadcasted_iota(jnp.int32, (2 * radii, radii), 0)
    column = lax.broadcasted_iota(jnp.int32, (2 * radii, radii), 1)
    doubling = jnp.where(row // 2 == column, 1.0, 0.0).astype(jnp.bfloat16)
    parity = lax.broadcasted_iota(jnp.int32, (2 * radii, packed), 0) % 2
    for fetch in fetches:
        fetch.wait()

    def one_part(c, carry):
        field = c // parts_count
        pltpu.make_async_copy(arrived.at[c], arrived.at[c], in_recv.at[c]).wait()
        rates = eigen_ref[pl.ds(field, 1), :]
        rates = jnp.transpose(jnp.broadcast_to(rates, (128, radii)))[:, 0:1]
        shrink = 1.0 + rates + diffusivity_ref[field] * harmonic
        values = arrived[c].reshape(radii, packed).astype(jnp.float32)
        turned = jnp.dot(
            left_ref[field], values, precision=lax.Precision.HIGHEST, preferred_element_type=jnp.float32
        )
        scaled = turned * (covered / shrink)
        result = jnp.dot(
            right_ref[field], scaled, precision=lax.Precision.HIGHEST, preferred_element_type=jnp.float32
        )
        doubled = jnp.dot(doubling, result.astype(jnp.bfloat16), preferred_element_type=jnp.float32)
        updated[...] = (doubled * jnp.where(parity == 0, live[0], live[1])).astype(jnp.bfloat16)
        for kb in range(modes):
            b = lax.rem(my_mode + kb, modes)
            columns = pl.ds(pl.multiple_of(b * lats, lats), lats)
            summed = jnp.dot(
                updated[...], polynomial_rows[:, columns], preferred_element_type=jnp.float32
            )
            blocks = summed.reshape(rads, rows, 2, lats).astype(jnp.bfloat16)
            for a in range(rads):
                held[(c * modes + kb) * rads + a] = blocks[a]
            for ka in far_first(rads):
                a = lax.rem(my_rad + ka, rads)
                source = held.at[(c * modes + kb) * rads + a]
                target = o_ref.at[c * devices + me]
                if ka or kb:
                    pltpu.make_async_remote_copy(
                        src_ref=source,
                        dst_ref=target,
                        send_sem=out_send,
                        recv_sem=out_recv,
                        device_id=(a, b),
                        device_id_type=MESH,
                    ).start()
                else:
                    pltpu.make_async_copy(source, target, out_local).start()
        return carry

    lax.fori_loop(0, parts, one_part, 0)
    others = arrived.at[:, pl.ds(0, rads - 1)]
    pltpu.make_async_copy(others, others, in_send).wait()
    remote = pl.ds(0, parts * (devices - 1))
    pltpu.make_async_copy(held.at[remote], held.at[remote], out_send).wait()
    pltpu.make_async_copy(o_ref.at[remote], o_ref.at[remote], out_recv).wait()
    own = pl.ds(0, parts)
    pltpu.make_async_copy(held.at[own], o_ref.at[own], out_local).wait()


PLANES = 4
EARLY = 2
PIECES = 4


def pieces_of(value, count):
    pieces = []
    for _ in range(count):
        piece = value.astype(jnp.bfloat16)
        pieces.append(piece)
        value = value - piece.astype(jnp.float32)
    return pieces


def product(left, right):
    return jnp.dot(left, right, preferred_element_type=jnp.float32)


def factored_kernel(
    rads,
    modes,
    parts_count,
    capacity,
    order_ref,
    start_ref,
    diffusivity_ref,
    eigen_ref,
    left_hbm,
    right_hbm,
    x_ref,
    legendre_ref,
    o_ref,
    flag_ref,
    left_ref,
    right_ref,
    entering,
    outgoing,
    arrived,
    polynomial_rows,
    solved,
    updated,
    updated_far,
    held,
    long_out,
    long_in,
    short_out,
    short_in,
    staged,
    pooled,
    packed_out,
    packed_in,
    table_out,
    table_in,
    table,
    enter_sem,
    in_send,
    in_recv,
    factor_sem,
    legendre_sem,
    table_send,
    table_recv,
    table_sem,
    stage_send,
    pool_recv,
    pack_send,
    pack_recv,
    relay_send,
    short_send,
    short_recv,
    spread_send,
    spread_recv,
    long_send,
    long_recv,
    out_send,
    out_recv,
    out_local,
    far_local,
):
    my_rad = lax.axis_index("rad")
    my_mode = lax.axis_index("mode")
    devices = rads * modes
    slots = entering.shape[0]
    parts = arrived.shape[0]
    packed = arrived.shape[3]
    radii = right_ref.shape[1]
    rows, columns = held.shape[1], held.shape[3]
    half = rads // 2
    across = rads // PLANES
    group_count = half * modes
    window_blocks = staged.shape[1]
    window = window_blocks * BLOCK
    width = staged.shape[3]
    me = my_rad * modes + my_mode
    side = my_rad // half
    near_base = side * half
    far_base = half - near_base
    gate_base = half - across + side * across
    far_gate_base = half - side * across
    outer_base = side * (rads - across)
    place = lax.rem(my_rad, across)
    plane_base = my_rad - place
    is_gate = plane_base == gate_base
    my_group = (my_rad - near_base) * modes + my_mode

    def remote(source, target, send_sem, recv_sem, rad, mode):
        return pltpu.make_async_remote_copy(
            src_ref=source,
            dst_ref=target,
            send_sem=send_sem,
            recv_sem=recv_sem,
            device_id=(rad, mode),
            device_id_type=MESH,
        )

    def enter(c):
        slot = lax.rem(c, slots)
        return pltpu.make_async_copy(x_ref.at[c], entering.at[slot], enter_sem.at[slot])

    for c in range(min(slots, parts)):
        enter(c).start()
    fetches = (
        pltpu.make_async_copy(left_hbm, left_ref, factor_sem.at[0]),
        pltpu.make_async_copy(right_hbm, right_ref, factor_sem.at[1]),
    )
    fetch_legendre = pltpu.make_async_copy(legendre_ref, polynomial_rows, legendre_sem)
    fetch_legendre.start()
    for fetch in fetches:
        fetch.start()
    barrier = pltpu.get_barrier_semaphore()
    for ka in range(rads):
        for kb in range(modes):
            if ka or kb:
                peer = (lax.rem(my_rad + ka, rads), lax.rem(my_mode + kb, modes))
                pl.semaphore_signal(barrier, inc=1, device_id=peer, device_id_type=MESH)

    blocks = [DEGREES // BLOCK - order_ref[0, 0, s] // BLOCK for s in range(2)]
    short = jnp.where(blocks[0] <= blocks[1], 0, 1)
    short_blocks = jnp.minimum(blocks[0], blocks[1])
    lane = lax.broadcasted_iota(jnp.int32, table_out.shape, 1)
    table_out[...] = jnp.where(lane == 0, short_blocks, jnp.where(lane == 1, short, 0))

    def turn(c):
        enter(c).wait()
        outgoing[c] = jnp.swapaxes(entering[lax.rem(c, slots)], 0, 1)

        @pl.when(c + slots < parts)
        def _():
            enter(c + slots).start()

    turn(0)
    pl.semaphore_wait(barrier, devices - 1)

    def send_part(c, carry):
        @pl.when(c > 0)
        def _():
            turn(c)

        for k in range(half):
            a = far_base + lax.rem(my_rad + k, half)
            remote(
                outgoing.at[c, a], arrived.at[c, my_rad], in_send, in_recv.at[c], a, my_mode
            ).start()
        for k in range(1, half):
            a = near_base + lax.rem(my_rad + k, half)
            remote(
                outgoing.at[c, a], arrived.at[c, my_rad], in_send, in_recv.at[c], a, my_mode
            ).start()
        pltpu.make_async_copy(outgoing.at[c, my_rad], arrived.at[c, my_rad], in_recv.at[c]).start()
        return carry

    lax.fori_loop(0, EARLY, send_part, 0)

    fetch_legendre.wait()
    for b in range(modes):
        for y in range(across):
            lats = slice(b * columns + y * width, b * columns + (y + 1) * width)
            leading = polynomial_rows[:window, lats]
            trailing = polynomial_rows[packed - window :, lats]
            chosen = jnp.where(short == 0, leading, trailing)
            staged[b * across + y] = chosen.reshape(window_blocks, BLOCK, width)
    for kb in range(modes):
        b = lax.rem(my_mode + kb, modes)
        for ky in range(across):
            y = lax.rem(place + ky, across)
            source = staged.at[b * across + y]
            target = pooled.at[my_group]
            if kb or ky:
                remote(source, target, stage_send, pool_recv, gate_base + y, b).start()
            else:

                @pl.when(is_gate)
                def _():
                    pltpu.make_async_copy(source, target, pool_recv).start()

                @pl.when(jnp.logical_not(is_gate))
                def _():
                    remote(source, target, stage_send, pool_recv, gate_base + y, b).start()

    for k in range(1, devices):
        d = lax.rem(me + k, devices)
        remote(
            table_out,
            table_in.at[me],
            table_send,
            table_recv,
            d // modes,
            lax.rem(d, modes),
        ).start()
    pltpu.make_async_copy(table_out, table_in.at[me], table_recv).start()

    lax.fori_loop(EARLY, parts, send_part, 0)

    position = lax.broadcasted_iota(jnp.int32, (1, packed), 1)
    live = []
    degree = jnp.zeros((1, packed), jnp.int32)
    for s in range(2):
        order = order_ref[0, 0, s]
        start = start_ref[0, 0, s]
        first_degree = BLOCK * (order // BLOCK)
        inside = (position >= start) & (position < start + DEGREES - first_degree)
        row_degree = first_degree + position - start
        degree = degree + jnp.where(inside, row_degree, 0)
        live.append(jnp.where(inside & (row_degree >= order), 1.0, 0.0).astype(jnp.float32))
    degree_level = degree.astype(jnp.float32)
    harmonic = degree_level * (degree_level + 1.0) / (DEGREES * DEGREES)
    covered = jnp.maximum(live[0], live[1])
    live_short = jnp.where(short == 0, live[0], live[1])
    live_long = jnp.where(short == 0, live[1], live[0])
    half_radii = half * rows
    row = lax.broadcasted_iota(jnp.int32, (2 * half_radii, half_radii), 0)
    column = lax.broadcasted_iota(jnp.int32, (2 * half_radii, half_radii), 1)
    doubling = jnp.where(row // 2 == column, 1.0, 0.0).astype(jnp.bfloat16)
    stretch = packed // 3 if packed % (3 * BLOCK) == 0 else packed
    parity = lax.broadcasted_iota(jnp.int32, (2 * half_radii, stretch), 0) % 2
    for fetch in fetches:
        fetch.wait()

    def send_long(c):
        for kb in range(modes):
            b = lax.rem(my_mode + kb, modes)
            for k in range(half):
                i = lax.rem(my_rad + k, half)
                remote(
                    long_out.at[c, b, i],
                    long_in.at[c, my_group],
                    long_send,
                    long_recv.at[c],
                    far_base + i,
                    b,
                ).start()

    def one_part(c, carry):
        field = c // parts_count
        pltpu.make_async_copy(arrived.at[c], arrived.at[c], in_recv.at[c]).wait()
        rates = eigen_ref[pl.ds(field, 1), :]
        rates = jnp.transpose(jnp.broadcast_to(rates, (128, radii)))[:, 0:1]
        left = pieces_of(left_ref[field], 3)
        right = pieces_of(right_ref[field], 2)
        for first in range(0, packed, stretch):
            cut = slice(first, first + stretch)
            shrink = 1.0 + rates + diffusivity_ref[field] * harmonic[:, cut]
            values = arrived[c, :, :, cut].reshape(radii, stretch)
            turned = product(left[2], values) + product(left[1], values) + product(left[0], values)
            high, low = pieces_of(turned * (covered[:, cut] / shrink), 2)
            result = product(right[0], low) + product(right[1], high) + product(right[0], high)
            solved[:, cut] = result.astype(jnp.bfloat16)

        far = solved[pl.ds(pl.multiple_of(far_base * rows, half_radii), half_radii), :]
        far = far.astype(jnp.float32)
        updated_far[...] = (far * live_long).astype(jnp.bfloat16)
        masked = (far * live_short).astype(jnp.bfloat16)
        masked = jnp.where(short == 0, masked[:, :window], masked[:, packed - window :])
        short_out[c] = masked.reshape(half, rows, window)
        for k in range(half):
            i = lax.rem(my_rad + k, half)
            remote(
                short_out.at[c, i],
                short_in.at[my_mode, c, my_rad - near_base],
                short_send,
                short_recv.at[c],
                far_base + i,
                my_mode,
            ).start()

        def far_mode(b, carry):
            lats = pl.ds(pl.multiple_of(b * columns, columns), columns)
            summed = product(updated_far[...], polynomial_rows[:, lats])
            long_out[c, b] = summed.astype(jnp.bfloat16).reshape(half, rows, columns)
            return carry

        lax.fori_loop(0, modes, far_mode, 0)

        @pl.when(c < EARLY)
        def _():
            send_long(c)

        for first in range(0, packed, stretch):
            cut = slice(first, first + stretch)
            near = solved[pl.ds(pl.multiple_of(near_base * rows, half_radii), half_radii), cut]
            doubled = product(doubling, near)
            chosen = jnp.where(parity == 0, live[0][:, cut], live[1][:, cut])
            updated[:, cut] = (doubled * chosen).astype(jnp.bfloat16)

        def near_mode(kb, carry):
            b = lax.rem(my_mode + kb, modes)
            lats = pl.ds(pl.multiple_of(b * columns, columns), columns)
            summed = product(updated[...], polynomial_rows[:, lats])
            block = (c * modes + kb) * half
            held[pl.ds(block, half)] = summed.reshape(half, rows, 2, columns).astype(jnp.bfloat16)
            target = o_ref.at[c * devices + me]
            for k in range(1, half):
                i = lax.rem(my_rad + k, half)
                remote(held.at[block + i], target, out_send, out_recv, near_base + i, b).start()
            source = held.at[block + my_rad - near_base]

            @pl.when(kb > 0)
            def _():
                remote(source, target, out_send, out_recv, my_rad, b).start()

            @pl.when(kb == 0)
            def _():
                pltpu.make_async_copy(source, target, out_local).start()

            return carry

        lax.fori_loop(0, modes, near_mode, 0)

        @pl.when(c == EARLY - 1)
        def _():
            gather()

        return carry

    piece = capacity // PIECES

    def gather():
        pltpu.make_async_copy(table_in, table_in, table_recv).wait()
        to_scalars = pltpu.make_async_copy(table_in, table, table_sem)
        to_scalars.start()
        to_scalars.wait()

        @pl.when(is_gate)
        def _():
            pltpu.make_async_copy(pooled, pooled, pool_recv).wait()
            spans = []
            offset = jnp.int32(0)
            for group in range(group_count):
                count = table[near_base * modes + group, 0, 0]
                first = jnp.where(
                    table[near_base * modes + group, 0, 1] == 0, 0, window_blocks - count
                )
                spans.append((offset, offset + count, first - offset))
                offset = offset + count

            def one_block(j, carry):
                group, block = jnp.int32(0), jnp.int32(0)
                for k, (begin, end, shift) in enumerate(spans):
                    inside = (j >= begin) & (j < end)
                    group = jnp.where(inside, k, group)
                    block = jnp.where(inside, j + shift, block)
                packed_out[j] = pooled[group, jnp.clip(block, 0, window_blocks - 1)]
                return carry

            def pack(p, carry):
                lax.fori_loop(p * piece, (p + 1) * piece, one_block, 0)
                some = pl.ds(p * piece, piece)
                remote(
                    packed_out.at[some],
                    packed_in.at[place, some],
                    pack_send,
                    pack_recv.at[place, p],
                    far_gate_base + place,
                    my_mode,
                ).start()
                return carry

            lax.fori_loop(0, PIECES, pack, 0)

    lax.fori_loop(0, parts, one_part, 0)

    def late_long(c, carry):
        send_long(c)
        return carry

    lax.fori_loop(EARLY, parts, late_long, 0)

    def arrived_piece(y, p):
        some = packed_in.at[y, pl.ds(p * piece, piece)]
        return pltpu.make_async_copy(some, some, pack_recv.at[y, p])

    def relay(p, carry):
        arrived_piece(place, p).wait()
        some = packed_in.at[place, pl.ds(p * piece, piece)]

        @pl.when(is_gate)
        def _():
            remote(
                some, some, relay_send, pack_recv.at[place, p], outer_base + place, my_mode
            ).start()

        for k in range(1, across):
            remote(
                some,
                some,
                relay_send,
                pack_recv.at[place, p],
                plane_base + lax.rem(place + k, across),
                my_mode,
            ).start()
        return carry

    def spread(c, carry):
        mine = short_in.at[my_mode, c]
        pltpu.make_async_copy(mine, mine, short_recv.at[c]).wait()
        for k in range(1, modes):
            b = lax.rem(my_mode + k, modes)
            remote(mine, mine, spread_send, spread_recv, my_rad, b).start()
        return carry

    lax.fori_loop(0, EARLY, spread, 0)
    lax.fori_loop(0, PIECES, relay, 0)
    lax.fori_loop(EARLY, parts, spread, 0)

    other_blocks = held.at[pl.ds(0, parts * (group_count - 1))]
    pltpu.make_async_copy(other_blocks, other_blocks, out_send).wait()
    own = pl.ds(0, parts)
    pltpu.make_async_copy(held.at[own], o_ref.at[own], out_local).wait()

    def arrived_pieces(p, carry):
        for k in range(1, across):
            arrived_piece(lax.rem(place + k, across), p).wait()
        return carry

    lax.fori_loop(0, PIECES, arrived_pieces, 0)
    others = short_in.at[pl.ds(0, modes - 1)]
    pltpu.make_async_copy(others, others, spread_recv).wait()

    per_group = parts * rows
    sent_parts = outgoing.at[:, pl.ds(0, rads - 1)]

    pltpu.make_async_copy(sent_parts, sent_parts, in_send).wait()
    counts = [table[far_base * modes + group, 0, 0] for group in range(group_count)]

    def one_group(group, carry):
        far_group = far_base * modes + group
        offset = jnp.int32(0)
        for k in range(group_count - 1):
            offset = offset + jnp.where(k < group, counts[k], 0)
        count = table[far_group, 0, 0]
        first = jnp.where(table[far_group, 0, 1] == 0, 0, window_blocks - count)
        factors = short_in[lax.rem(group, modes), :, group // modes].reshape(per_group, window)
        for y in range(across):
            taken = []
            for w in range(window_blocks):
                j = jnp.clip(offset + w - first, 0, capacity - 1)
                taken.append(packed_in[y, j])
            summed = product(factors, jnp.concatenate(taken, axis=0))
            lats = pl.ds(
                pl.multiple_of((group // rads) * columns + y * width, width), width
            )
            outgoing[:, lax.rem(group, rads), :, lats] = summed.reshape(parts, rows, width).astype(
                jnp.bfloat16
            )
        return carry

    lax.fori_loop(0, group_count, one_group, 0)

    together = 4
    size = 2 * together * rows
    row = lax.broadcasted_iota(jnp.int32, (size, size), 0)
    column = lax.broadcasted_iota(jnp.int32, (size, size), 1)
    origin = (row % 2) * (together * rows) + (row // (2 * rows)) * rows + (row % (2 * rows)) // 2
    merging = jnp.where(column == origin, 1.0, 0.0).astype(jnp.bfloat16)

    def merge_part(c, carry):
        pltpu.make_async_copy(long_in.at[c], long_in.at[c], long_recv.at[c]).wait()

        def merge_some(q, carry):
            for y in range(across):
                lats = slice(y * width, (y + 1) * width)
                leading, trailing = [], []
                for k in range(together):
                    group = q * together + k
                    taken = pl.ds(
                        pl.multiple_of((group // rads) * columns + y * width, width), width
                    )
                    from_short = outgoing[c, lax.rem(group, rads), :, taken]
                    from_long = long_in[c, group, :, lats]
                    short_first = table[far_base * modes + group, 0, 1] == 0
                    leading.append(jnp.where(short_first, from_short, from_long))
                    trailing.append(jnp.where(short_first, from_long, from_short))
                merged = product(merging, jnp.concatenate(leading + trailing, axis=0))
                block = pl.ds(c * group_count + q * together, together)
                held[block, :, :, lats] = merged.reshape(together, rows, 2, width).astype(
                    jnp.bfloat16
                )
            return carry

        lax.fori_loop(0, group_count // together, merge_some, 0)
        pltpu.make_async_copy(
            held.at[pl.ds(c * group_count, group_count)],
            o_ref.at[pl.ds(c * devices + far_base * modes, group_count)],
            far_local,
        ).start()
        return carry

    lax.fori_loop(0, parts, merge_part, 0)

    low, high = jnp.int32(0), jnp.int32(0)
    for group in range(group_count):
        low = low + table[group, 0, 0]
        high = high + table[group_count + group, 0, 0]
    flag_ref[0, 0] = jnp.where(jnp.maximum(low, high) > capacity, 1, 0)

    sent = table_in.at[pl.ds(0, devices - 1)]
    pltpu.make_async_copy(sent, sent, table_send).wait()
    sent = staged.at[pl.ds(0, modes * across - 1)]
    pltpu.make_async_copy(sent, sent, stage_send).wait()
    pltpu.make_async_copy(short_out, short_out, short_send).wait()
    pltpu.make_async_copy(others, others, spread_send).wait()
    pltpu.make_async_copy(long_out, long_out, long_send).wait()

    @pl.when(is_gate)
    def _():
        pltpu.make_async_copy(packed_out, packed_out, pack_send).wait()
        pltpu.make_async_copy(packed_out, packed_out, relay_send).wait()

    @pl.when(jnp.logical_not(is_gate))
    def _():
        pltpu.make_async_copy(staged.at[0], staged.at[0], stage_send).wait()

    for k in range(1, across):
        pltpu.make_async_copy(packed_in.at[0], packed_in.at[0], relay_send).wait()
    remote_blocks = o_ref.at[pl.ds(0, parts * (group_count - 1))]
    pltpu.make_async_copy(remote_blocks, remote_blocks, out_recv).wait()
    far_blocks = pl.ds(0, parts * group_count)
    pltpu.make_async_copy(held.at[far_blocks], o_ref.at[far_blocks], far_local).wait()


def factored(rads, modes, capacity, arguments):
    (
        coefficients,
        legendre,
        radial_left_factor,
        radial_right,
        eigen_rates,
        diffusivity,
        slot_order,
        slot_start,
    ) = arguments
    packed, lats = legendre.shape[2:]
    radii = radial_right.shape[1]
    fields, parts_count = coefficients.shape[:2]
    parts = fields * parts_count
    devices = rads * modes
    rows, columns = radii // rads, lats // modes
    half, across = rads // 2, rads // PLANES
    groups, width = half * modes, columns // across
    window = packed // BLOCK // 2 * BLOCK
    smem = pl.BlockSpec(memory_space=pltpu.SMEM)
    vmem = pl.BlockSpec(memory_space=pltpu.VMEM)
    hbm = pl.BlockSpec(memory_space=pltpu.HBM)
    kept = jnp.bfloat16
    dma = pltpu.SemaphoreType.DMA
    return pl.pallas_call(
        functools.partial(factored_kernel, rads, modes, parts_count, capacity),
        out_shape=(
            pltpu.VMEM((parts * devices, rows, 2, columns), kept),
            jax.ShapeDtypeStruct((1, 1), jnp.int32),
        ),
        in_specs=[smem, smem, smem, vmem, hbm, hbm, hbm, hbm],
        out_specs=(pl.BlockSpec(memory_space=pl.ANY), smem),
        scratch_shapes=[
            pltpu.VMEM(radial_left_factor.shape, jnp.float32),
            pltpu.VMEM(radial_right.shape, jnp.float32),
            pltpu.VMEM((min(3, parts), rows, rads, packed), kept),
            pltpu.VMEM((parts, rads, rows, packed), kept),
            pltpu.VMEM((parts, rads, rows, packed), kept),
            pltpu.VMEM((packed, lats), kept),
            pltpu.VMEM((radii, packed), kept),
            pltpu.VMEM((radii, packed), kept),
            pltpu.VMEM((radii // 2, packed), kept),
            pltpu.VMEM((parts * groups, rows, 2, columns), kept),
            pltpu.VMEM((parts, modes, half, rows, columns), kept),
            pltpu.VMEM((parts, groups, rows, columns), kept),
            pltpu.VMEM((parts, half, rows, window), kept),
            pltpu.VMEM((modes, parts, half, rows, window), kept),
            pltpu.VMEM((modes * across, window // BLOCK, BLOCK, width), kept),
            pltpu.VMEM((groups, window // BLOCK, BLOCK, width), kept),
            pltpu.VMEM((capacity, BLOCK, width), kept),
            pltpu.VMEM((across, capacity, BLOCK, width), kept),
            pltpu.VMEM((8, 128), jnp.int32),
            pltpu.VMEM((devices, 8, 128), jnp.int32),
            pltpu.SMEM((devices, 8, 128), jnp.int32),
            dma((min(3, parts),)),
            dma,
            dma((parts,)),
            dma((2,)),
            dma,
            dma,
            dma,
            dma,
            dma,
            dma,
            dma,
            dma((across, PIECES)),
            dma,
            dma,
            dma((parts,)),
            dma,
            dma,
            dma,
            dma((parts,)),
            dma,
            dma,
            dma,
            dma,
        ],
        compiler_params=pltpu.CompilerParams(
            collective_id=1, has_side_effects=True, vmem_limit_bytes=50 * 2**20
        ),
    )(
        slot_order,
        slot_start,
        diffusivity,
        eigen_rates,
        radial_left_factor,
        radial_right,
        coefficients.reshape(parts, rows, rads, packed),
        legendre.reshape(packed, lats),
    )


def dense(
    rads,
    modes,
    arguments,
):
    (
        coefficients,
        legendre,
        radial_left_factor,
        radial_right,
        eigen_rates,
        diffusivity,
        slot_order,
        slot_start,
    ) = arguments
    packed, lats = legendre.shape[2:]
    radii = radial_right.shape[1]
    fields, parts_count = coefficients.shape[:2]
    parts = fields * parts_count
    devices = rads * modes
    rows, columns = radii // rads, lats // modes
    smem = pl.BlockSpec(memory_space=pltpu.SMEM)
    vmem = pl.BlockSpec(memory_space=pltpu.VMEM)
    hbm = pl.BlockSpec(memory_space=pltpu.HBM)
    return pl.pallas_call(
        functools.partial(whole_kernel, rads, modes, parts_count),
        out_shape=pltpu.VMEM((parts * devices, rows, 2, columns), jnp.bfloat16),
        in_specs=[smem, smem, smem, vmem, hbm, hbm, hbm, hbm],
        out_specs=pl.BlockSpec(memory_space=pl.ANY),
        scratch_shapes=[
            pltpu.VMEM(radial_left_factor.shape, jnp.float32),
            pltpu.VMEM(radial_right.shape, jnp.float32),
            pltpu.VMEM((parts, rows, rads, packed), jnp.bfloat16),
            pltpu.VMEM((parts, rads, rows, packed), jnp.bfloat16),
            pltpu.VMEM((parts, rads, rows, packed), jnp.bfloat16),
            pltpu.VMEM((packed, lats), jnp.bfloat16),
            pltpu.VMEM((2 * radii, packed), jnp.bfloat16),
            pltpu.VMEM((parts * devices, rows, 2, columns), jnp.bfloat16),
            pltpu.SemaphoreType.DMA((parts,)),
            pltpu.SemaphoreType.DMA,
            pltpu.SemaphoreType.DMA((parts,)),
            pltpu.SemaphoreType.DMA((2,)),
            pltpu.SemaphoreType.DMA,
            pltpu.SemaphoreType.DMA,
            pltpu.SemaphoreType.DMA,
            pltpu.SemaphoreType.DMA,
        ],
        compiler_params=pltpu.CompilerParams(
            collective_id=0, has_side_effects=True, vmem_limit_bytes=46 * 2**20
        ),
    )(
        slot_order,
        slot_start,
        diffusivity,
        eigen_rates,
        radial_left_factor,
        radial_right,
        coefficients.reshape(parts, rows, rads, packed),
        legendre.reshape(packed, lats),
    )


def on_device(rads, modes, *arguments):
    coefficients, legendre, _, radial_right = arguments[:4]
    packed, lats = legendre.shape[2:]
    rows, columns = radial_right.shape[1] // rads, lats // modes
    fields, parts_count = coefficients.shape[:2]
    parts = fields * parts_count
    half, across = rads // 2, rads // PLANES
    groups = half * modes
    window_blocks = packed // BLOCK // 2
    capacity = 3 * groups * window_blocks // 4
    fits = (
        rads % PLANES == 0
        and columns % (BLOCK * across) == 0
        and groups <= rads * (packed // columns)
        and across * capacity * BLOCK * (columns // across) <= 2**22
    )
    if fits:
        landed, flag = factored(rads, modes, capacity, arguments)
        landed = lax.cond(
            flag[0, 0] > 0, lambda: dense(rads, modes, arguments), lambda: landed
        )
    else:
        landed = dense(rads, modes, arguments)
    return landed.reshape(fields, parts_count, rads, modes, rows, 2, columns)


def solution(mesh):
    rads, modes = mesh.shape["rad"], mesh.shape["mode"]
    return jax.shard_map(
        functools.partial(on_device, rads, modes),
        mesh=mesh,
        in_specs=(
            P(None, None, "rad", None, "mode", None),
            P("rad", "mode", None, None),
            P(),
            P(),
            P(),
            P(),
            P("rad", "mode", None),
            P("rad", "mode", None),
        ),
        out_specs=P(None, None, None, None, "rad", None, "mode"),
        check_vma=False,
    )
```

```python
import functools
import jax
import jax.numpy as jnp
from jax import lax
from jax.experimental import pallas as pl
from jax.experimental.pallas import tpu as pltpu
from jax.sharding import PartitionSpec as P

DEGREES = 1024
BLOCK = 128
MESH = pl.DeviceIdType.MESH


def far_first(count):
    return sorted(range(count), key=lambda k: (-min(k, count - k), k))


def whole_kernel(
    rads,
    modes,
    parts_count,
    order_ref,
    start_ref,
    diffusivity_ref,
    eigen_ref,
    left_hbm,
    right_hbm,
    x_ref,
    legendre_ref,
    o_ref,
    left_ref,
    right_ref,
    entering,
    outgoing,
    arrived,
    polynomial_rows,
    updated,
    held,
    enter_sem,
    in_send,
    in_recv,
    factor_sem,
    legendre_sem,
    out_send,
    out_recv,
    out_local,
):
    my_rad = lax.axis_index("rad")
    my_mode = lax.axis_index("mode")
    devices = rads * modes
    parts = arrived.shape[0]
    packed = arrived.shape[3]
    radii = right_ref.shape[1]
    rows, lats = held.shape[1], held.shape[3]
    me = my_rad * modes + my_mode

    def enter(c):
        return pltpu.make_async_copy(x_ref.at[c], entering.at[c], enter_sem.at[c])

    for c in range(parts):
        enter(c).start()
    fetches = (
        pltpu.make_async_copy(left_hbm, left_ref, factor_sem.at[0]),
        pltpu.make_async_copy(right_hbm, right_ref, factor_sem.at[1]),
        pltpu.make_async_copy(legendre_ref, polynomial_rows, legendre_sem),
    )
    for fetch in fetches:
        fetch.start()
    barrier = pltpu.get_barrier_semaphore()
    for ka in range(rads):
        for kb in range(modes):
            if ka or kb:
                peer = (lax.rem(my_rad + ka, rads), lax.rem(my_mode + kb, modes))
                pl.semaphore_signal(barrier, inc=1, device_id=peer, device_id_type=MESH)

    def turn(c):
        enter(c).wait()
        outgoing[c] = jnp.swapaxes(entering[c], 0, 1)

    turn(0)
    pl.semaphore_wait(barrier, devices - 1)

    def send_part(c, carry):
        @pl.when(c > 0)
        def _():
            turn(c)

        for ka in far_first(rads):
            a = lax.rem(my_rad + ka, rads)
            source = outgoing.at[c, a]
            target = arrived.at[c, my_rad]
            if ka:
                pltpu.make_async_remote_copy(
                    src_ref=source,
                    dst_ref=target,
                    send_sem=in_send,
                    recv_sem=in_recv.at[c],
                    device_id=(a, my_mode),
                    device_id_type=MESH,
                ).start()
            else:
                pltpu.make_async_copy(source, target, in_recv.at[c]).start()
        return carry

    lax.fori_loop(0, parts, send_part, 0)

    position = lax.broadcasted_iota(jnp.int32, (1, packed), 1)
    live = []
    degree = jnp.zeros((1, packed), jnp.int32)
    for s in range(2):
        order = order_ref[0, 0, s]
        start = start_ref[0, 0, s]
        first_degree = BLOCK * (order // BLOCK)
        inside = (position >= start) & (position < start + DEGREES - first_degree)
        row_degree = first_degree + position - start
        degree = degree + jnp.where(inside, row_degree, 0)
        live.append(jnp.where(inside & (row_degree >= order), 1.0, 0.0).astype(jnp.float32))
    degree_level = degree.astype(jnp.float32)
    harmonic = degree_level * (degree_level + 1.0) / (DEGREES * DEGREES)
    covered = jnp.maximum(live[0], live[1])
    row = lax.broadcasted_iota(jnp.int32, (2 * radii, radii), 0)
    column = lax.broadcasted_iota(jnp.int32, (2 * radii, radii), 1)
    doubling = jnp.where(row // 2 == column, 1.0, 0.0).astype(jnp.bfloat16)
    parity = lax.broadcasted_iota(jnp.int32, (2 * radii, packed), 0) % 2
    for fetch in fetches:
        fetch.wait()

    def one_part(c, carry):
        field = c // parts_count
        pltpu.make_async_copy(arrived.at[c], arrived.at[c], in_recv.at[c]).wait()
        rates = eigen_ref[pl.ds(field, 1), :]
        rates = jnp.transpose(jnp.broadcast_to(rates, (128, radii)))[:, 0:1]
        shrink = 1.0 + rates + diffusivity_ref[field] * harmonic
        values = arrived[c].reshape(radii, packed).astype(jnp.float32)
        turned = jnp.dot(
            left_ref[field], values, precision=lax.Precision.HIGHEST, preferred_element_type=jnp.float32
        )
        scaled = turned * (covered / shrink)
        result = jnp.dot(
            right_ref[field], scaled, precision=lax.Precision.HIGHEST, preferred_element_type=jnp.float32
        )
        doubled = jnp.dot(doubling, result.astype(jnp.bfloat16), preferred_element_type=jnp.float32)
        updated[...] = (doubled * jnp.where(parity == 0, live[0], live[1])).astype(jnp.bfloat16)
        for kb in range(modes):
            b = lax.rem(my_mode + kb, modes)
            columns = pl.ds(pl.multiple_of(b * lats, lats), lats)
            summed = jnp.dot(
                updated[...], polynomial_rows[:, columns], preferred_element_type=jnp.float32
            )
            blocks = summed.reshape(rads, rows, 2, lats).astype(jnp.bfloat16)
            for a in range(rads):
                held[(c * modes + kb) * rads + a] = blocks[a]
            for ka in far_first(rads):
                a = lax.rem(my_rad + ka, rads)
                source = held.at[(c * modes + kb) * rads + a]
                target = o_ref.at[c * devices + me]
                if ka or kb:
                    pltpu.make_async_remote_copy(
                        src_ref=source,
                        dst_ref=target,
                        send_sem=out_send,
                        recv_sem=out_recv,
                        device_id=(a, b),
                        device_id_type=MESH,
                    ).start()
                else:
                    pltpu.make_async_copy(source, target, out_local).start()
        return carry

    lax.fori_loop(0, parts, one_part, 0)
    others = arrived.at[:, pl.ds(0, rads - 1)]
    pltpu.make_async_copy(others, others, in_send).wait()
    remote = pl.ds(0, parts * (devices - 1))
    pltpu.make_async_copy(held.at[remote], held.at[remote], out_send).wait()
    pltpu.make_async_copy(o_ref.at[remote], o_ref.at[remote], out_recv).wait()
    own = pl.ds(0, parts)
    pltpu.make_async_copy(held.at[own], o_ref.at[own], out_local).wait()


PLANES = 4
EARLY = 2
SHORT_AFTER = 2
PIECES = 4
UNIT = 16


def pieces_of(value, count):
    pieces = []
    for _ in range(count):
        piece = value.astype(jnp.bfloat16)
        pieces.append(piece)
        value = value - piece.astype(jnp.float32)
    return pieces


def product(left, right):
    return jnp.dot(left, right, preferred_element_type=jnp.float32)


def factored_kernel(
    rads,
    modes,
    parts_count,
    unit_room,
    block_room,
    order_ref,
    start_ref,
    diffusivity_ref,
    eigen_ref,
    left_hbm,
    right_hbm,
    x_ref,
    legendre_ref,
    o_ref,
    flag_ref,
    left_ref,
    right_ref,
    entering,
    outgoing,
    arrived,
    polynomial_rows,
    updated,
    updated_far,
    held,
    long_out,
    long_in,
    short_out,
    short_pooled,
    short_packed_out,
    short_packed_in,
    staged,
    pooled,
    packed_out,
    packed_in,
    table_out,
    table_in,
    table,
    order_out,
    order_in,
    enter_sem,
    in_send,
    in_recv,
    factor_sem,
    legendre_sem,
    table_send,
    table_recv,
    table_sem,
    stage_send,
    pool_recv,
    pack_send,
    pack_recv,
    relay_send,
    short_send,
    short_pool_recv,
    short_pack_send,
    short_pack_recv,
    spread_send,
    long_send,
    long_recv,
    out_send,
    out_recv,
    out_local,
    far_local,
):
    my_rad = lax.axis_index("rad")
    my_mode = lax.axis_index("mode")
    devices = rads * modes
    slots = entering.shape[0]
    parts = arrived.shape[0]
    packed = arrived.shape[3]
    radii = right_ref.shape[1]
    rows, columns = held.shape[1], held.shape[3]
    half = rads // 2
    across = rads // PLANES
    group_count = half * modes
    window_units = staged.shape[1]
    window_blocks = window_units * UNIT // BLOCK
    window = window_units * UNIT
    shares = short_out.shape[1]
    share_parts = parts // shares
    width = staged.shape[3]
    me = my_rad * modes + my_mode
    side = my_rad // half
    near_base = side * half
    far_base = half - near_base
    gate_base = half - across + side * across
    far_gate_base = half - side * across
    outer_base = side * (rads - across)
    place = lax.rem(my_rad, across)
    plane_base = my_rad - place
    is_gate = plane_base == gate_base
    my_group = (my_rad - near_base) * modes + my_mode

    def remote(source, target, send_sem, recv_sem, rad, mode):
        return pltpu.make_async_remote_copy(
            src_ref=source,
            dst_ref=target,
            send_sem=send_sem,
            recv_sem=recv_sem,
            device_id=(rad, mode),
            device_id_type=MESH,
        )

    def enter(c):
        slot = lax.rem(c, slots)
        return pltpu.make_async_copy(x_ref.at[c], entering.at[slot], enter_sem.at[slot])

    for c in range(min(slots, parts)):
        enter(c).start()
    fetches = (
        pltpu.make_async_copy(left_hbm, left_ref, factor_sem.at[0]),
        pltpu.make_async_copy(right_hbm, right_ref, factor_sem.at[1]),
    )
    fetch_legendre = pltpu.make_async_copy(legendre_ref, polynomial_rows, legendre_sem)
    fetch_legendre.start()
    for fetch in fetches:
        fetch.start()
    barrier = pltpu.get_barrier_semaphore()
    for ka in range(rads):
        for kb in range(modes):
            if ka or kb:
                peer = (lax.rem(my_rad + ka, rads), lax.rem(my_mode + kb, modes))
                pl.semaphore_signal(barrier, inc=1, device_id=peer, device_id_type=MESH)

    blocks = [DEGREES // BLOCK - order_ref[0, 0, s] // BLOCK for s in range(2)]
    short = jnp.where(blocks[0] <= blocks[1], 0, 1)
    short_blocks = jnp.minimum(jnp.minimum(blocks[0], blocks[1]), window_blocks)
    short_order = jnp.where(short == 0, order_ref[0, 0, 0], order_ref[0, 0, 1])
    unused = (short_order - BLOCK * (short_order // BLOCK)) // UNIT
    short_units = short_blocks * (BLOCK // UNIT) - unused
    lane = lax.broadcasted_iota(jnp.int32, table_out.shape, 1)
    entries = jnp.where(lane == 2, short_units, 0)
    entries = jnp.where(lane == 1, short, entries)
    table_out[...] = jnp.where(lane == 0, short_blocks, entries)

    def extent(device):
        count = table[device, 0, 0]
        short_first = table[device, 0, 1] == 0
        units = table[device, 0, 2]
        first = jnp.where(short_first, 0, window_blocks - count)
        first_unit = jnp.where(short_first, count * (BLOCK // UNIT) - units, window_units - units)
        return count, first, units, first_unit

    def turn(c):
        enter(c).wait()
        outgoing[c] = jnp.swapaxes(entering[lax.rem(c, slots)], 0, 1)

        @pl.when(c + slots < parts)
        def _():
            enter(c + slots).start()

    turn(0)
    pl.semaphore_wait(barrier, devices - 1)

    def send_part(c, carry):
        @pl.when(c > 0)
        def _():
            turn(c)

        for k in range(half):
            a = far_base + lax.rem(my_rad + k, half)
            remote(
                outgoing.at[c, a], arrived.at[c, my_rad], in_send, in_recv.at[c], a, my_mode
            ).start()
        for k in range(1, half):
            a = near_base + lax.rem(my_rad + k, half)
            remote(
                outgoing.at[c, a], arrived.at[c, my_rad], in_send, in_recv.at[c], a, my_mode
            ).start()
        pltpu.make_async_copy(outgoing.at[c, my_rad], arrived.at[c, my_rad], in_recv.at[c]).start()
        return carry

    lax.fori_loop(0, 1, send_part, 0)
    for k in range(1, devices):
        d = lax.rem(me + k, devices)
        remote(
            table_out,
            table_in.at[me],
            table_send,
            table_recv,
            d // modes,
            lax.rem(d, modes),
        ).start()
    pltpu.make_async_copy(table_out, table_in.at[me], table_recv).start()

    lax.fori_loop(1, EARLY, send_part, 0)

    fetch_legendre.wait()
    for b in range(modes):
        for y in range(across):
            lats = slice(b * columns + y * width, b * columns + (y + 1) * width)
            leading = polynomial_rows[:window, lats]
            trailing = polynomial_rows[packed - window :, lats]
            chosen = jnp.where(short == 0, leading, trailing)
            staged[b * across + y] = chosen.reshape(window_units, UNIT, width)
    for kb in range(modes):
        b = lax.rem(my_mode + kb, modes)
        for ky in range(across):
            y = lax.rem(place + ky, across)
            source = staged.at[b * across + y]
            target = pooled.at[my_group]
            if kb or ky:
                remote(source, target, stage_send, pool_recv, gate_base + y, b).start()
            else:

                @pl.when(is_gate)
                def _():
                    pltpu.make_async_copy(source, target, pool_recv).start()

                @pl.when(jnp.logical_not(is_gate))
                def _():
                    remote(source, target, stage_send, pool_recv, gate_base + y, b).start()

    lax.fori_loop(EARLY, parts, send_part, 0)

    position = lax.broadcasted_iota(jnp.int32, (1, packed), 1)
    live = []
    degree = jnp.zeros((1, packed), jnp.int32)
    for s in range(2):
        order = order_ref[0, 0, s]
        start = start_ref[0, 0, s]
        first_degree = BLOCK * (order // BLOCK)
        inside = (position >= start) & (position < start + DEGREES - first_degree)
        row_degree = first_degree + position - start
        degree = degree + jnp.where(inside, row_degree, 0)
        live.append(jnp.where(inside & (row_degree >= order), 1.0, 0.0).astype(jnp.float32))
    degree_level = degree.astype(jnp.float32)
    harmonic = degree_level * (degree_level + 1.0) / (DEGREES * DEGREES)
    covered = jnp.maximum(live[0], live[1])
    live_short = jnp.where(short == 0, live[0], live[1])
    live_long = jnp.where(short == 0, live[1], live[0])
    half_radii = half * rows
    row = lax.broadcasted_iota(jnp.int32, (2 * half_radii, half_radii), 0)
    column = lax.broadcasted_iota(jnp.int32, (2 * half_radii, half_radii), 1)
    doubling = jnp.where(row // 2 == column, 1.0, 0.0).astype(jnp.bfloat16)
    stretch = packed // 3 if packed % (3 * BLOCK) == 0 else packed
    parity = lax.broadcasted_iota(jnp.int32, (2 * half_radii, stretch), 0) % 2
    for fetch in fetches:
        fetch.wait()

    def send_long(c):
        for kb in range(modes):
            b = lax.rem(my_mode + kb, modes)
            for k in range(half):
                i = lax.rem(my_rad + k, half)
                remote(
                    long_out.at[c, b, i],
                    long_in.at[c, my_group],
                    long_send,
                    long_recv.at[c, my_rad - near_base],
                    far_base + i,
                    b,
                ).start()

    def one_part(c, carry):
        field = c // parts_count
        pltpu.make_async_copy(arrived.at[c], arrived.at[c], in_recv.at[c]).wait()
        rates = eigen_ref[pl.ds(field, 1), :]
        rates = jnp.transpose(jnp.broadcast_to(rates, (128, radii)))[:, 0:1]
        left = pieces_of(left_ref[field], 3)
        right = pieces_of(right_ref[field], 2)
        for first in range(0, packed, stretch):
            cut = slice(first, first + stretch)
            shrink = 1.0 + rates + diffusivity_ref[field] * harmonic[:, cut]
            values = arrived[c, :, :, cut].reshape(radii, stretch)
            turned = product(left[2], values) + product(left[1], values) + product(left[0], values)
            high, low = pieces_of(turned * (covered[:, cut] / shrink), 2)
            result = product(right[0], low) + product(right[1], high) + product(right[0], high)
            arrived[c, :, :, cut] = result.astype(jnp.bfloat16).reshape(rads, rows, stretch)

        far = arrived[c, pl.ds(far_base, half)].reshape(half_radii, packed).astype(jnp.float32)
        masked = (far * live_short).astype(jnp.bfloat16)
        masked = jnp.where(short == 0, masked[:, :window], masked[:, packed - window :])
        share, place_in_share = c // share_parts, lax.rem(c, share_parts)
        for i in range(half):
            for w in range(window_blocks):
                short_out[i, share, w, place_in_share] = masked[
                    i * rows : (i + 1) * rows, w * BLOCK : (w + 1) * BLOCK
                ]

        @pl.when(place_in_share == share_parts - 1)
        def _():
            for k in range(half):
                i = lax.rem(my_rad + k, half)
                y = lax.rem(i, across)
                b = i // across * shares + share
                source, target = short_out.at[i, share], short_pooled.at[my_group]
                local = is_gate & (y == place) & (b == my_mode)

                @pl.when(local)
                def _():
                    pltpu.make_async_copy(source, target, short_pool_recv).start()

                @pl.when(jnp.logical_not(local))
                def _():
                    remote(source, target, short_send, short_pool_recv, gate_base + y, b).start()

        @pl.when(c < EARLY)
        def _():
            far_part(c)

        @pl.when(is_gate)
        def _():
            near_part(c)

        @pl.when(c == EARLY - 1)
        def _():
            gather()

        return carry

    def far_part(c):
        far = arrived[c, pl.ds(far_base, half)].reshape(half_radii, packed).astype(jnp.float32)
        updated_far[...] = (far * live_long).astype(jnp.bfloat16)

        def far_mode(b, carry):
            lats = pl.ds(pl.multiple_of(b * columns, columns), columns)
            summed = product(updated_far[...], polynomial_rows[:, lats])
            long_out[c, b] = summed.astype(jnp.bfloat16).reshape(half, rows, columns)
            return carry

        lax.fori_loop(0, modes, far_mode, 0)
        send_long(c)

    def near_part(c):
        for first in range(0, packed, stretch):
            cut = slice(first, first + stretch)
            near = arrived[c, pl.ds(near_base, half), :, cut]
            doubled = product(doubling, near.reshape(half_radii, stretch))
            chosen = jnp.where(parity == 0, live[0][:, cut], live[1][:, cut])
            updated[:, cut] = (doubled * chosen).astype(jnp.bfloat16)

        def near_mode(kb, carry):
            b = lax.rem(my_mode + kb, modes)
            lats = pl.ds(pl.multiple_of(b * columns, columns), columns)
            summed = product(updated[...], polynomial_rows[:, lats])
            block = (c * modes + kb) * half
            held[pl.ds(block, half)] = summed.reshape(half, rows, 2, columns).astype(jnp.bfloat16)
            target = o_ref.at[c * devices + me]
            for k in range(1, half):
                i = lax.rem(my_rad + k, half)
                remote(held.at[block + i], target, out_send, out_recv, near_base + i, b).start()
            source = held.at[block + my_rad - near_base]

            @pl.when(kb > 0)
            def _():
                remote(source, target, out_send, out_recv, my_rad, b).start()

            @pl.when(kb == 0)
            def _():
                pltpu.make_async_copy(source, target, out_local).start()

            return carry

        lax.fori_loop(0, modes, near_mode, 0)

    piece = unit_room // PIECES
    short_piece = block_room // PIECES
    ahead = (packed_in.shape[1] - unit_room) // 2

    def gather():
        pltpu.make_async_copy(table_in, table_in, table_recv).wait()
        to_scalars = pltpu.make_async_copy(table_in, table, table_sem)
        to_scalars.start()
        to_scalars.wait()

        @pl.when(is_gate)
        def _():
            shape = order_out.shape[1:]
            index = BLOCK * lax.broadcasted_iota(jnp.int32, shape, 0) + lax.broadcasted_iota(
                jnp.int32, shape, 1
            )
            unit_source = jnp.zeros(shape, jnp.int32)
            block_source = jnp.zeros(shape, jnp.int32)
            unit_offset, block_offset = jnp.int32(0), jnp.int32(0)
            for group in range(group_count):
                count, first, units, first_unit = extent(near_base * modes + group)
                inside = (index >= unit_offset) & (index < unit_offset + units)
                shift = group * window_units + first_unit - unit_offset
                unit_source = jnp.where(inside, index + shift, unit_source)
                inside = (index >= block_offset) & (index < block_offset + count)
                shift = group * window_blocks + first - block_offset
                block_source = jnp.where(inside, index + shift, block_source)
                unit_offset = unit_offset + units
                block_offset = block_offset + count
            order_out[0] = unit_source
            order_out[1] = block_source
            to_scalars = pltpu.make_async_copy(order_out, order_in, table_sem)
            to_scalars.start()
            pltpu.make_async_copy(pooled, pooled, pool_recv).wait()
            to_scalars.wait()

            def one_unit(j, carry):
                source = order_in[0, j // BLOCK, lax.rem(j, BLOCK)]
                group = jnp.clip(source // window_units, 0, group_count - 1)
                unit = jnp.clip(source - group * window_units, 0, window_units - 1)
                packed_out[j] = pooled[group, unit]
                return carry

            def pack(p, carry):
                lax.fori_loop(p * piece, (p + 1) * piece, one_unit, 0)
                remote(
                    packed_out.at[pl.ds(p * piece, piece)],
                    packed_in.at[place, pl.ds(ahead + p * piece, piece)],
                    pack_send,
                    pack_recv.at[place, p],
                    far_gate_base + place,
                    my_mode,
                ).start()
                return carry

            lax.fori_loop(0, PIECES, pack, 0)

    def gather_short():
        pltpu.make_async_copy(short_pooled, short_pooled, short_pool_recv).wait()

        def one_block(j, carry):
            source = order_in[1, j // BLOCK, lax.rem(j, BLOCK)]
            group = jnp.clip(source // window_blocks, 0, group_count - 1)
            block = jnp.clip(source - group * window_blocks, 0, window_blocks - 1)
            short_packed_out[j] = short_pooled[group, block]
            return carry

        def pack(p, carry):
            lax.fori_loop(p * short_piece, (p + 1) * short_piece, one_block, 0)
            some = pl.ds(p * short_piece, short_piece)
            remote(
                short_packed_out.at[some],
                short_packed_in.at[lax.rem(my_mode, shares), some],
                short_pack_send,
                short_pack_recv.at[lax.rem(my_mode, shares), p],
                far_base + my_mode // shares * across + place,
                my_mode,
            ).start()
            return carry

        lax.fori_loop(0, PIECES, pack, 0)

    blank = jnp.zeros((ahead, UNIT, width), jnp.bfloat16)
    for y in range(across):
        packed_in[y, :ahead] = blank
        packed_in[y, ahead + unit_room :] = blank

    lax.fori_loop(0, parts, one_part, 0)

    def arrived_piece(y, p):
        some = packed_in.at[y, pl.ds(ahead + p * piece, piece)]
        return pltpu.make_async_copy(some, some, pack_recv.at[y, p])

    def relay(p, carry):
        arrived_piece(place, p).wait()
        some = packed_in.at[place, pl.ds(ahead + p * piece, piece)]

        @pl.when(is_gate)
        def _():
            remote(
                some, some, relay_send, pack_recv.at[place, p], outer_base + place, my_mode
            ).start()

        for k in range(1, across):
            remote(
                some,
                some,
                relay_send,
                pack_recv.at[place, p],
                plane_base + lax.rem(place + k, across),
                my_mode,
            ).start()
        return carry

    def short_piece_of(share, p):
        some = short_packed_in.at[share, pl.ds(p * short_piece, short_piece)]
        return pltpu.make_async_copy(some, some, short_pack_recv.at[share, p])

    my_share = lax.rem(my_mode, shares)
    is_spreader = my_mode // shares == (my_rad - near_base) // across

    def spread(p, carry):
        short_piece_of(my_share, p).wait()
        some = short_packed_in.at[my_share, pl.ds(p * short_piece, short_piece)]
        arrival = short_pack_recv.at[my_share, p]

        @pl.when(is_spreader)
        def _():
            for k in range(shares, modes, shares):
                mate = lax.rem(my_mode + k, modes)
                remote(some, some, spread_send, arrival, my_rad, mate).start()

        for k in range(1, shares):
            sibling = my_mode - my_share + lax.rem(my_share + k, shares)
            remote(some, some, spread_send, arrival, my_rad, sibling).start()
        return carry

    def late_part(c, carry):
        @pl.when(c >= EARLY)
        def _():
            far_part(c)

        @pl.when(jnp.logical_not(is_gate))
        def _():
            near_part(c)

        @pl.when((c == SHORT_AFTER) & is_gate)
        def _():
            lax.fori_loop(0, PIECES // 2, relay, 0)
            gather_short()
            lax.fori_loop(PIECES // 2, PIECES, relay, 0)

        return carry

    lax.fori_loop(0, parts, late_part, 0)

    @pl.when(jnp.logical_not(is_gate))
    def _():
        lax.fori_loop(0, PIECES, relay, 0)

    lax.fori_loop(0, PIECES, spread, 0)

    other_blocks = held.at[pl.ds(0, parts * (group_count - 1))]
    pltpu.make_async_copy(other_blocks, other_blocks, out_send).wait()
    own = pl.ds(0, parts)
    pltpu.make_async_copy(held.at[own], o_ref.at[own], out_local).wait()

    def arrived_pieces(p, carry):
        for k in range(1, across):
            arrived_piece(lax.rem(place + k, across), p).wait()
        return carry

    lax.fori_loop(0, PIECES, arrived_pieces, 0)

    def arrived_shorts(p, carry):
        for k in range(1, shares):
            short_piece_of(lax.rem(my_mode + k, shares), p).wait()

        return carry

    lax.fori_loop(0, PIECES, arrived_shorts, 0)

    sent_parts = outgoing.at[:, pl.ds(0, rads - 1)]

    pltpu.make_async_copy(sent_parts, sent_parts, in_send).wait()
    counts = [table[far_base * modes + group, 0, 0] for group in range(group_count)]
    units_of = [table[far_base * modes + group, 0, 2] for group in range(group_count)]

    def one_group(group, carry):
        count, first, _, first_unit = extent(far_base * modes + group)
        offset, unit_offset = jnp.int32(0), jnp.int32(0)
        for k in range(group_count - 1):
            offset = offset + jnp.where(k < group, counts[k], 0)
            unit_offset = unit_offset + jnp.where(k < group, units_of[k], 0)
        factors = []
        for share in range(shares):
            taken = []
            for w in range(window_blocks):
                j = jnp.clip(offset + w - first, 0, block_room - 1)
                block = short_packed_in[share, j].reshape(share_parts * rows, BLOCK)
                valid = (w >= first) & (w < first + count)
                taken.append(jnp.where(valid, block, jnp.zeros_like(block)))
            factors.append(jnp.concatenate(taken, axis=1))
        factors = jnp.concatenate(factors, axis=0)
        begin = jnp.clip(ahead + unit_offset - first_unit, 0, ahead + unit_room)
        for y in range(across):
            taken = [packed_in[y, begin + k] for k in range(window_units)]
            summed = product(factors, jnp.concatenate(taken, axis=0))
            lats = pl.ds(
                pl.multiple_of((group // rads) * columns + y * width, width), width
            )
            outgoing[:, lax.rem(group, rads), :, lats] = summed.reshape(parts, rows, width).astype(
                jnp.bfloat16
            )
        return carry

    lax.fori_loop(0, group_count, one_group, 0)

    together = modes
    size = 2 * together * rows
    row = lax.broadcasted_iota(jnp.int32, (size, size), 0)
    column = lax.broadcasted_iota(jnp.int32, (size, size), 1)
    origin = (row % 2) * (together * rows) + (row // (2 * rows)) * rows + (row % (2 * rows)) // 2
    merging = jnp.where(column == origin, 1.0, 0.0).astype(jnp.bfloat16)

    def merge_part(c, carry):
        def merge_some(q, carry):
            row_groups = long_in.at[c, pl.ds(q * together, together)]
            pltpu.make_async_copy(row_groups, row_groups, long_recv.at[c, q]).wait()
            for y in range(across):
                lats = slice(y * width, (y + 1) * width)
                leading, trailing = [], []
                for k in range(together):
                    group = q * together + k
                    taken = pl.ds(
                        pl.multiple_of((group // rads) * columns + y * width, width), width
                    )
                    from_short = outgoing[c, lax.rem(group, rads), :, taken]
                    from_long = long_in[c, group, :, lats]
                    short_first = table[far_base * modes + group, 0, 1] == 0
                    leading.append(jnp.where(short_first, from_short, from_long))
                    trailing.append(jnp.where(short_first, from_long, from_short))
                merged = product(merging, jnp.concatenate(leading + trailing, axis=0))
                block = pl.ds(c * group_count + q * together, together)
                held[block, :, :, lats] = merged.reshape(together, rows, 2, width).astype(
                    jnp.bfloat16
                )
            pltpu.make_async_copy(
                held.at[pl.ds(c * group_count + q * together, together)],
                o_ref.at[pl.ds(c * devices + far_base * modes + q * together, together)],
                far_local,
            ).start()
            return carry

        lax.fori_loop(0, group_count // together, merge_some, 0)
        return carry

    lax.fori_loop(0, parts, merge_part, 0)

    overfull = jnp.int32(0)
    for begin in (0, group_count):
        blocks_used, units_used = jnp.int32(0), jnp.int32(0)
        for group in range(begin, begin + group_count):
            blocks_used = blocks_used + table[group, 0, 0]
            units_used = units_used + table[group, 0, 2]
        overfull = jnp.where((blocks_used > block_room) | (units_used > unit_room), 1, overfull)
    flag_ref[0, 0] = overfull

    sent = table_in.at[pl.ds(0, devices - 1)]
    pltpu.make_async_copy(sent, sent, table_send).wait()
    sent = staged.at[pl.ds(0, modes * across - 1)]
    pltpu.make_async_copy(sent, sent, stage_send).wait()
    for share in range(shares):
        for i in range(half):
            sent = short_out.at[i, share]
            local = is_gate & (i % across == place) & (i // across * shares + share == my_mode)

            @pl.when(jnp.logical_not(local))
            def _():
                pltpu.make_async_copy(sent, sent, short_send).wait()

    for k in range(1, shares):
        pltpu.make_async_copy(short_packed_out, short_packed_out, spread_send).wait()

    @pl.when(is_spreader)
    def _():
        for k in range(shares, modes, shares):
            pltpu.make_async_copy(short_packed_out, short_packed_out, spread_send).wait()

    pltpu.make_async_copy(long_out, long_out, long_send).wait()

    @pl.when(is_gate)
    def _():
        pltpu.make_async_copy(packed_out, packed_out, pack_send).wait()
        pltpu.make_async_copy(packed_out, packed_out, relay_send).wait()
        pltpu.make_async_copy(short_packed_out, short_packed_out, short_pack_send).wait()

    @pl.when(jnp.logical_not(is_gate))
    def _():
        pltpu.make_async_copy(staged.at[0], staged.at[0], stage_send).wait()

    for k in range(1, across):
        pltpu.make_async_copy(packed_out, packed_out, relay_send).wait()
    remote_blocks = o_ref.at[pl.ds(0, parts * (group_count - 1))]
    pltpu.make_async_copy(remote_blocks, remote_blocks, out_recv).wait()
    far_blocks = pl.ds(0, parts * group_count)
    pltpu.make_async_copy(held.at[far_blocks], o_ref.at[far_blocks], far_local).wait()


def factored(rads, modes, unit_room, block_room, arguments):
    (
        coefficients,
        legendre,
        radial_left_factor,
        radial_right,
        eigen_rates,
        diffusivity,
        slot_order,
        slot_start,
    ) = arguments
    packed, lats = legendre.shape[2:]
    radii = radial_right.shape[1]
    fields, parts_count = coefficients.shape[:2]
    parts = fields * parts_count
    devices = rads * modes
    rows, columns = radii // rads, lats // modes
    half, across = rads // 2, rads // PLANES
    groups, width = half * modes, columns // across
    window = packed // BLOCK // 2 * BLOCK
    shares = 2 * modes // PLANES
    smem = pl.BlockSpec(memory_space=pltpu.SMEM)
    vmem = pl.BlockSpec(memory_space=pltpu.VMEM)
    hbm = pl.BlockSpec(memory_space=pltpu.HBM)
    kept = jnp.bfloat16
    dma = pltpu.SemaphoreType.DMA
    return pl.pallas_call(
        functools.partial(factored_kernel, rads, modes, parts_count, unit_room, block_room),
        out_shape=(
            pltpu.VMEM((parts * devices, rows, 2, columns), kept),
            jax.ShapeDtypeStruct((1, 1), jnp.int32),
        ),
        in_specs=[smem, smem, smem, vmem, hbm, hbm, hbm, hbm],
        out_specs=(pl.BlockSpec(memory_space=pl.ANY), smem),
        scratch_shapes=[
            pltpu.VMEM(radial_left_factor.shape, jnp.float32),
            pltpu.VMEM(radial_right.shape, jnp.float32),
            pltpu.VMEM((min(3, parts), rows, rads, packed), kept),
            pltpu.VMEM((parts, rads, rows, packed), kept),
            pltpu.VMEM((parts, rads, rows, packed), kept),
            pltpu.VMEM((packed, lats), kept),
            pltpu.VMEM((radii, packed), kept),
            pltpu.VMEM((radii // 2, packed), kept),
            pltpu.VMEM((parts * groups, rows, 2, columns), kept),
            pltpu.VMEM((parts, modes, half, rows, columns), kept),
            pltpu.VMEM((parts, groups, rows, columns), kept),
            pltpu.VMEM((half, shares, window // BLOCK, parts // shares, rows, BLOCK), kept),
            pltpu.VMEM((groups, window // BLOCK, parts // shares, rows, BLOCK), kept),
            pltpu.VMEM((block_room, parts // shares, rows, BLOCK), kept),
            pltpu.VMEM((shares, block_room, parts // shares, rows, BLOCK), kept),
            pltpu.VMEM((modes * across, window // UNIT, UNIT, width), kept),
            pltpu.VMEM((groups, window // UNIT, UNIT, width), kept),
            pltpu.VMEM((unit_room, UNIT, width), kept),
            pltpu.VMEM((across, unit_room + 2 * window // UNIT, UNIT, width), kept),
            pltpu.VMEM((8, 128), jnp.int32),
            pltpu.VMEM((devices, 8, 128), jnp.int32),
            pltpu.SMEM((devices, 8, 128), jnp.int32),
            pltpu.VMEM((2, 8, 128), jnp.int32),
            pltpu.SMEM((2, 8, 128), jnp.int32),
            dma((min(3, parts),)),
            dma,
            dma((parts,)),
            dma((2,)),
            dma,
            dma,
            dma,
            dma,
            dma,
            dma,
            dma,
            dma((across, PIECES)),
            dma,
            dma,
            dma,
            dma,
            dma((shares, PIECES)),
            dma,
            dma,
            dma((parts, half)),
            dma,
            dma,
            dma,
            dma,
        ],
        compiler_params=pltpu.CompilerParams(
            collective_id=1, has_side_effects=True, vmem_limit_bytes=50 * 2**20
        ),
    )(
        slot_order,
        slot_start,
        diffusivity,
        eigen_rates,
        radial_left_factor,
        radial_right,
        coefficients.reshape(parts, rows, rads, packed),
        legendre.reshape(packed, lats),
    )


def dense(
    rads,
    modes,
    arguments,
):
    (
        coefficients,
        legendre,
        radial_left_factor,
        radial_right,
        eigen_rates,
        diffusivity,
        slot_order,
        slot_start,
    ) = arguments
    packed, lats = legendre.shape[2:]
    radii = radial_right.shape[1]
    fields, parts_count = coefficients.shape[:2]
    parts = fields * parts_count
    devices = rads * modes
    rows, columns = radii // rads, lats // modes
    smem = pl.BlockSpec(memory_space=pltpu.SMEM)
    vmem = pl.BlockSpec(memory_space=pltpu.VMEM)
    hbm = pl.BlockSpec(memory_space=pltpu.HBM)
    return pl.pallas_call(
        functools.partial(whole_kernel, rads, modes, parts_count),
        out_shape=pltpu.VMEM((parts * devices, rows, 2, columns), jnp.bfloat16),
        in_specs=[smem, smem, smem, vmem, hbm, hbm, hbm, hbm],
        out_specs=pl.BlockSpec(memory_space=pl.ANY),
        scratch_shapes=[
            pltpu.VMEM(radial_left_factor.shape, jnp.float32),
            pltpu.VMEM(radial_right.shape, jnp.float32),
            pltpu.VMEM((parts, rows, rads, packed), jnp.bfloat16),
            pltpu.VMEM((parts, rads, rows, packed), jnp.bfloat16),
            pltpu.VMEM((parts, rads, rows, packed), jnp.bfloat16),
            pltpu.VMEM((packed, lats), jnp.bfloat16),
            pltpu.VMEM((2 * radii, packed), jnp.bfloat16),
            pltpu.VMEM((parts * devices, rows, 2, columns), jnp.bfloat16),
            pltpu.SemaphoreType.DMA((parts,)),
            pltpu.SemaphoreType.DMA,
            pltpu.SemaphoreType.DMA((parts,)),
            pltpu.SemaphoreType.DMA((2,)),
            pltpu.SemaphoreType.DMA,
            pltpu.SemaphoreType.DMA,
            pltpu.SemaphoreType.DMA,
            pltpu.SemaphoreType.DMA,
        ],
        compiler_params=pltpu.CompilerParams(
            collective_id=0, has_side_effects=True, vmem_limit_bytes=46 * 2**20
        ),
    )(
        slot_order,
        slot_start,
        diffusivity,
        eigen_rates,
        radial_left_factor,
        radial_right,
        coefficients.reshape(parts, rows, rads, packed),
        legendre.reshape(packed, lats),
    )


def on_device(rads, modes, *arguments):
    coefficients, legendre, _, radial_right = arguments[:4]
    packed, lats = legendre.shape[2:]
    rows, columns = radial_right.shape[1] // rads, lats // modes
    fields, parts_count = coefficients.shape[:2]
    parts = fields * parts_count
    half, across = rads // 2, rads // PLANES
    groups = half * modes
    window_blocks = packed // BLOCK // 2
    window_units = window_blocks * BLOCK // UNIT
    block_room = 3 * groups * window_blocks // 4
    unit_room = 21 * groups * window_units // 32
    shares = 2 * modes // PLANES
    fits = (
        rads % PLANES == 0
        and 2 * modes % PLANES == 0
        and parts % max(shares, 1) == 0
        and columns % (BLOCK * across) == 0
        and groups <= rads * (packed // columns)
        and unit_room % PIECES == 0
        and unit_room <= 8 * BLOCK
        and across * unit_room * UNIT * (columns // across) <= 2**22
    )
    if fits:
        landed, flag = factored(rads, modes, unit_room, block_room, arguments)
        landed = lax.switch(
            flag[0, 0], (lambda: landed, lambda: dense(rads, modes, arguments))
        )
    else:
        landed = dense(rads, modes, arguments)
    return landed.reshape(fields, parts_count, rads, modes, rows, 2, columns)


def solution(mesh):
    rads, modes = mesh.shape["rad"], mesh.shape["mode"]
    return jax.shard_map(
        functools.partial(on_device, rads, modes),
        mesh=mesh,
        in_specs=(
            P(None, None, "rad", None, "mode", None),
            P("rad", "mode", None, None),
            P(),
            P(),
            P(),
            P(),
            P("rad", "mode", None),
            P("rad", "mode", None),
        ),
        out_specs=P(None, None, None, None, "rad", None, "mode"),
        check_vma=False,
    )
```

```python
import functools
import jax
import jax.numpy as jnp
from jax import lax
from jax.experimental import pallas as pl
from jax.experimental.pallas import tpu as pltpu
from jax.sharding import PartitionSpec as P

DEGREES = 1024
BLOCK = 128
MESH = pl.DeviceIdType.MESH


def far_first(count):
    return sorted(range(count), key=lambda k: (-min(k, count - k), k))


def whole_kernel(
    rads,
    modes,
    parts_count,
    order_ref,
    start_ref,
    diffusivity_ref,
    eigen_ref,
    left_hbm,
    right_hbm,
    x_ref,
    legendre_ref,
    o_ref,
    left_ref,
    right_ref,
    entering,
    outgoing,
    arrived,
    polynomial_rows,
    updated,
    held,
    enter_sem,
    in_send,
    in_recv,
    factor_sem,
    legendre_sem,
    out_send,
    out_recv,
    out_local,
):
    my_rad = lax.axis_index("rad")
    my_mode = lax.axis_index("mode")
    devices = rads * modes
    parts = arrived.shape[0]
    packed = arrived.shape[3]
    radii = right_ref.shape[1]
    rows, lats = held.shape[1], held.shape[3]
    me = my_rad * modes + my_mode

    def enter(c):
        return pltpu.make_async_copy(x_ref.at[c], entering.at[c], enter_sem.at[c])

    for c in range(parts):
        enter(c).start()
    fetches = (
        pltpu.make_async_copy(left_hbm, left_ref, factor_sem.at[0]),
        pltpu.make_async_copy(right_hbm, right_ref, factor_sem.at[1]),
        pltpu.make_async_copy(legendre_ref, polynomial_rows, legendre_sem),
    )
    for fetch in fetches:
        fetch.start()
    barrier = pltpu.get_barrier_semaphore()
    for ka in range(rads):
        for kb in range(modes):
            if ka or kb:
                peer = (lax.rem(my_rad + ka, rads), lax.rem(my_mode + kb, modes))
                pl.semaphore_signal(barrier, inc=1, device_id=peer, device_id_type=MESH)

    def turn(c):
        enter(c).wait()
        outgoing[c] = jnp.swapaxes(entering[c], 0, 1)

    turn(0)
    pl.semaphore_wait(barrier, devices - 1)

    def send_part(c, carry):
        @pl.when(c > 0)
        def _():
            turn(c)

        for ka in far_first(rads):
            a = lax.rem(my_rad + ka, rads)
            source = outgoing.at[c, a]
            target = arrived.at[c, my_rad]
            if ka:
                pltpu.make_async_remote_copy(
                    src_ref=source,
                    dst_ref=target,
                    send_sem=in_send,
                    recv_sem=in_recv.at[c],
                    device_id=(a, my_mode),
                    device_id_type=MESH,
                ).start()
            else:
                pltpu.make_async_copy(source, target, in_recv.at[c]).start()
        return carry

    lax.fori_loop(0, parts, send_part, 0)

    position = lax.broadcasted_iota(jnp.int32, (1, packed), 1)
    live = []
    degree = jnp.zeros((1, packed), jnp.int32)
    for s in range(2):
        order = order_ref[0, 0, s]
        start = start_ref[0, 0, s]
        first_degree = BLOCK * (order // BLOCK)
        inside = (position >= start) & (position < start + DEGREES - first_degree)
        row_degree = first_degree + position - start
        degree = degree + jnp.where(inside, row_degree, 0)
        live.append(jnp.where(inside & (row_degree >= order), 1.0, 0.0).astype(jnp.float32))
    degree_level = degree.astype(jnp.float32)
    harmonic = degree_level * (degree_level + 1.0) / (DEGREES * DEGREES)
    covered = jnp.maximum(live[0], live[1])
    row = lax.broadcasted_iota(jnp.int32, (2 * radii, radii), 0)
    column = lax.broadcasted_iota(jnp.int32, (2 * radii, radii), 1)
    doubling = jnp.where(row // 2 == column, 1.0, 0.0).astype(jnp.bfloat16)
    parity = lax.broadcasted_iota(jnp.int32, (2 * radii, packed), 0) % 2
    for fetch in fetches:
        fetch.wait()

    def one_part(c, carry):
        field = c // parts_count
        pltpu.make_async_copy(arrived.at[c], arrived.at[c], in_recv.at[c]).wait()
        rates = eigen_ref[pl.ds(field, 1), :]
        rates = jnp.transpose(jnp.broadcast_to(rates, (128, radii)))[:, 0:1]
        shrink = 1.0 + rates + diffusivity_ref[field] * harmonic
        values = arrived[c].reshape(radii, packed).astype(jnp.float32)
        turned = jnp.dot(
            left_ref[field], values, precision=lax.Precision.HIGHEST, preferred_element_type=jnp.float32
        )
        scaled = turned * (covered / shrink)
        result = jnp.dot(
            right_ref[field], scaled, precision=lax.Precision.HIGHEST, preferred_element_type=jnp.float32
        )
        doubled = jnp.dot(doubling, result.astype(jnp.bfloat16), preferred_element_type=jnp.float32)
        updated[...] = (doubled * jnp.where(parity == 0, live[0], live[1])).astype(jnp.bfloat16)
        for kb in range(modes):
            b = lax.rem(my_mode + kb, modes)
            columns = pl.ds(pl.multiple_of(b * lats, lats), lats)
            summed = jnp.dot(
                updated[...], polynomial_rows[:, columns], preferred_element_type=jnp.float32
            )
            blocks = summed.reshape(rads, rows, 2, lats).astype(jnp.bfloat16)
            for a in range(rads):
                held[(c * modes + kb) * rads + a] = blocks[a]
            for ka in far_first(rads):
                a = lax.rem(my_rad + ka, rads)
                source = held.at[(c * modes + kb) * rads + a]
                target = o_ref.at[c * devices + me]
                if ka or kb:
                    pltpu.make_async_remote_copy(
                        src_ref=source,
                        dst_ref=target,
                        send_sem=out_send,
                        recv_sem=out_recv,
                        device_id=(a, b),
                        device_id_type=MESH,
                    ).start()
                else:
                    pltpu.make_async_copy(source, target, out_local).start()
        return carry

    lax.fori_loop(0, parts, one_part, 0)
    others = arrived.at[:, pl.ds(0, rads - 1)]
    pltpu.make_async_copy(others, others, in_send).wait()
    remote = pl.ds(0, parts * (devices - 1))
    pltpu.make_async_copy(held.at[remote], held.at[remote], out_send).wait()
    pltpu.make_async_copy(o_ref.at[remote], o_ref.at[remote], out_recv).wait()
    own = pl.ds(0, parts)
    pltpu.make_async_copy(held.at[own], o_ref.at[own], out_local).wait()


PLANES = 4
EARLY = 2
SHORT_AFTER = 2
PIECES = 4
UNIT = 16


def pieces_of(value, count):
    pieces = []
    for _ in range(count):
        piece = value.astype(jnp.bfloat16)
        pieces.append(piece)
        value = value - piece.astype(jnp.float32)
    return pieces


def product(left, right):
    return jnp.dot(left, right, preferred_element_type=jnp.float32)


def factored_kernel(
    rads,
    modes,
    parts_count,
    unit_room,
    block_room,
    order_hbm,
    start_hbm,
    diffusivity_hbm,
    eigen_hbm,
    left_hbm,
    right_hbm,
    x_ref,
    legendre_ref,
    o_ref,
    flag_ref,
    order_ref,
    start_ref,
    diffusivity_ref,
    eigen_ref,
    left_ref,
    right_ref,
    entering,
    outgoing,
    arrived,
    polynomial_rows,
    updated,
    updated_far,
    held,
    long_out,
    long_in,
    short_out,
    short_pooled,
    short_packed_out,
    short_packed_in,
    staged,
    pooled,
    packed_out,
    packed_in,
    table_out,
    table_in,
    table,
    order_out,
    order_in,
    enter_sem,
    in_send,
    in_recv,
    factor_sem,
    legendre_sem,
    table_send,
    table_recv,
    table_sem,
    stage_send,
    pool_recv,
    pack_send,
    pack_recv,
    relay_send,
    short_send,
    short_pool_recv,
    short_pack_send,
    short_pack_recv,
    spread_send,
    long_send,
    long_recv,
    out_send,
    out_recv,
    out_local,
    far_local,
    setting_sem,
):
    my_rad = lax.axis_index("rad")
    my_mode = lax.axis_index("mode")
    devices = rads * modes
    slots = entering.shape[0]
    parts = arrived.shape[0]
    packed = arrived.shape[3]
    radii = right_ref.shape[1]
    rows, columns = held.shape[1], held.shape[3]
    half = rads // 2
    across = rads // PLANES
    group_count = half * modes
    window_units = staged.shape[1]
    window_blocks = window_units * UNIT // BLOCK
    window = window_units * UNIT
    shares = short_out.shape[1]
    share_parts = parts // shares
    width = staged.shape[3]
    me = my_rad * modes + my_mode
    side = my_rad // half
    near_base = side * half
    far_base = half - near_base
    gate_base = half - across + side * across
    far_gate_base = half - side * across
    outer_base = side * (rads - across)
    place = lax.rem(my_rad, across)
    plane_base = my_rad - place
    is_gate = plane_base == gate_base
    my_group = (my_rad - near_base) * modes + my_mode

    def remote(source, target, send_sem, recv_sem, rad, mode):
        return pltpu.make_async_remote_copy(
            src_ref=source,
            dst_ref=target,
            send_sem=send_sem,
            recv_sem=recv_sem,
            device_id=(rad, mode),
            device_id_type=MESH,
        )

    barrier = pltpu.get_barrier_semaphore()
    for ka in range(rads):
        for kb in range(modes):
            if ka or kb:
                peer = (lax.rem(my_rad + ka, rads), lax.rem(my_mode + kb, modes))
                pl.semaphore_signal(barrier, inc=1, device_id=peer, device_id_type=MESH)

    def enter(c):
        slot = lax.rem(c, slots)
        return pltpu.make_async_copy(x_ref.at[c], entering.at[slot], enter_sem.at[slot])

    settings = (
        pltpu.make_async_copy(order_hbm, order_ref, setting_sem.at[0]),
        pltpu.make_async_copy(start_hbm, start_ref, setting_sem.at[1]),
        pltpu.make_async_copy(diffusivity_hbm, diffusivity_ref, setting_sem.at[2]),
        pltpu.make_async_copy(eigen_hbm, eigen_ref, setting_sem.at[3]),
    )
    enter(0).start()
    for setting in settings:
        setting.start()
    for c in range(1, min(slots, parts)):
        enter(c).start()
    fetches = (
        pltpu.make_async_copy(left_hbm, left_ref, factor_sem.at[0]),
        pltpu.make_async_copy(right_hbm, right_ref, factor_sem.at[1]),
    )
    fetch_legendre = pltpu.make_async_copy(legendre_ref, polynomial_rows, legendre_sem)
    fetch_legendre.start()
    for fetch in fetches:
        fetch.start()

    def extent(device):
        count = table[device, 0, 0]
        short_first = table[device, 0, 1] == 0
        units = table[device, 0, 2]
        first = jnp.where(short_first, 0, window_blocks - count)
        first_unit = jnp.where(short_first, count * (BLOCK // UNIT) - units, window_units - units)
        return count, first, units, first_unit

    def turn(c):
        enter(c).wait()
        outgoing[c] = jnp.swapaxes(entering[lax.rem(c, slots)], 0, 1)

        @pl.when(c + slots < parts)
        def _():
            enter(c + slots).start()

    turn(0)
    settings[0].wait()

    blocks = [DEGREES // BLOCK - order_ref[0, 0, s] // BLOCK for s in range(2)]
    short = jnp.where(blocks[0] <= blocks[1], 0, 1)
    short_blocks = jnp.minimum(jnp.minimum(blocks[0], blocks[1]), window_blocks)
    short_order = jnp.where(short == 0, order_ref[0, 0, 0], order_ref[0, 0, 1])
    unused = (short_order - BLOCK * (short_order // BLOCK)) // UNIT
    short_units = short_blocks * (BLOCK // UNIT) - unused
    lane = lax.broadcasted_iota(jnp.int32, table_out.shape, 1)
    entries = jnp.where(lane == 2, short_units, 0)
    entries = jnp.where(lane == 1, short, entries)
    table_out[...] = jnp.where(lane == 0, short_blocks, entries)

    pl.semaphore_wait(barrier, devices - 1)

    def send_part(c, carry):
        @pl.when(c > 0)
        def _():
            turn(c)

        for k in range(half):
            a = far_base + lax.rem(my_rad + k, half)
            remote(
                outgoing.at[c, a], arrived.at[c, my_rad], in_send, in_recv.at[c], a, my_mode
            ).start()
        for k in range(1, half):
            a = near_base + lax.rem(my_rad + k, half)
            remote(
                outgoing.at[c, a], arrived.at[c, my_rad], in_send, in_recv.at[c], a, my_mode
            ).start()
        pltpu.make_async_copy(outgoing.at[c, my_rad], arrived.at[c, my_rad], in_recv.at[c]).start()
        return carry

    lax.fori_loop(0, 1, send_part, 0)
    for k in range(1, devices):
        d = lax.rem(me + k, devices)
        remote(
            table_out,
            table_in.at[me],
            table_send,
            table_recv,
            d // modes,
            lax.rem(d, modes),
        ).start()
    pltpu.make_async_copy(table_out, table_in.at[me], table_recv).start()

    lax.fori_loop(1, EARLY, send_part, 0)

    fetch_legendre.wait()
    for b in range(modes):
        for y in range(across):
            lats = slice(b * columns + y * width, b * columns + (y + 1) * width)
            leading = polynomial_rows[:window, lats]
            trailing = polynomial_rows[packed - window :, lats]
            chosen = jnp.where(short == 0, leading, trailing)
            staged[b * across + y] = chosen.reshape(window_units, UNIT, width)
    for kb in range(modes):
        b = lax.rem(my_mode + kb, modes)
        for ky in range(across):
            y = lax.rem(place + ky, across)
            source = staged.at[b * across + y]
            target = pooled.at[my_group]
            if kb or ky:
                remote(source, target, stage_send, pool_recv, gate_base + y, b).start()
            else:

                @pl.when(is_gate)
                def _():
                    pltpu.make_async_copy(source, target, pool_recv).start()

                @pl.when(jnp.logical_not(is_gate))
                def _():
                    remote(source, target, stage_send, pool_recv, gate_base + y, b).start()

    lax.fori_loop(EARLY, parts, send_part, 0)

    for setting in settings[1:]:
        setting.wait()
    position = lax.broadcasted_iota(jnp.int32, (1, packed), 1)
    live = []
    degree = jnp.zeros((1, packed), jnp.int32)
    for s in range(2):
        order = order_ref[0, 0, s]
        start = start_ref[0, 0, s]
        first_degree = BLOCK * (order // BLOCK)
        inside = (position >= start) & (position < start + DEGREES - first_degree)
        row_degree = first_degree + position - start
        degree = degree + jnp.where(inside, row_degree, 0)
        live.append(jnp.where(inside & (row_degree >= order), 1.0, 0.0).astype(jnp.float32))
    degree_level = degree.astype(jnp.float32)
    harmonic = degree_level * (degree_level + 1.0) / (DEGREES * DEGREES)
    covered = jnp.maximum(live[0], live[1])
    live_short = jnp.where(short == 0, live[0], live[1])
    live_long = jnp.where(short == 0, live[1], live[0])
    half_radii = half * rows
    row = lax.broadcasted_iota(jnp.int32, (2 * half_radii, half_radii), 0)
    column = lax.broadcasted_iota(jnp.int32, (2 * half_radii, half_radii), 1)
    doubling = jnp.where(row // 2 == column, 1.0, 0.0).astype(jnp.bfloat16)
    stretch = packed // 3 if packed % (3 * BLOCK) == 0 else packed
    parity = lax.broadcasted_iota(jnp.int32, (2 * half_radii, stretch), 0) % 2
    for fetch in fetches:
        fetch.wait()

    def send_long(c):
        for kb in range(modes):
            b = lax.rem(my_mode + kb, modes)
            for k in range(half):
                i = lax.rem(my_rad + k, half)
                remote(
                    long_out.at[c, b, i],
                    long_in.at[c, my_group],
                    long_send,
                    long_recv.at[c, my_rad - near_base],
                    far_base + i,
                    b,
                ).start()

    def one_part(c, carry):
        field = c // parts_count
        pltpu.make_async_copy(arrived.at[c], arrived.at[c], in_recv.at[c]).wait()
        rates = eigen_ref[pl.ds(field, 1), :]
        rates = jnp.transpose(jnp.broadcast_to(rates, (128, radii)))[:, 0:1]
        left = pieces_of(left_ref[field], 3)
        right = pieces_of(right_ref[field], 2)
        for first in range(0, packed, stretch):
            cut = slice(first, first + stretch)
            shrink = 1.0 + rates + diffusivity_ref[field] * harmonic[:, cut]
            values = arrived[c, :, :, cut].reshape(radii, stretch)
            turned = product(left[2], values) + product(left[1], values) + product(left[0], values)
            high, low = pieces_of(turned * (covered[:, cut] / shrink), 2)
            result = product(right[0], low) + product(right[1], high) + product(right[0], high)
            arrived[c, :, :, cut] = result.astype(jnp.bfloat16).reshape(rads, rows, stretch)

        far = arrived[c, pl.ds(far_base, half)].reshape(half_radii, packed).astype(jnp.float32)
        masked = (far * live_short).astype(jnp.bfloat16)
        masked = jnp.where(short == 0, masked[:, :window], masked[:, packed - window :])
        share, place_in_share = c // share_parts, lax.rem(c, share_parts)
        for i in range(half):
            for w in range(window_blocks):
                short_out[i, share, w, place_in_share] = masked[
                    i * rows : (i + 1) * rows, w * BLOCK : (w + 1) * BLOCK
                ]

        @pl.when(place_in_share == share_parts - 1)
        def _():
            for k in range(half):
                i = lax.rem(my_rad + k, half)
                y = lax.rem(i, across)
                b = i // across * shares + share
                source, target = short_out.at[i, share], short_pooled.at[my_group]
                local = is_gate & (y == place) & (b == my_mode)

                @pl.when(local)
                def _():
                    pltpu.make_async_copy(source, target, short_pool_recv).start()

                @pl.when(jnp.logical_not(local))
                def _():
                    remote(source, target, short_send, short_pool_recv, gate_base + y, b).start()

        @pl.when(c < EARLY)
        def _():
            far_part(c)

        @pl.when(is_gate)
        def _():
            near_part(c)

        @pl.when(c == EARLY - 1)
        def _():
            gather()

        return carry

    def far_part(c):
        far = arrived[c, pl.ds(far_base, half)].reshape(half_radii, packed).astype(jnp.float32)
        updated_far[...] = (far * live_long).astype(jnp.bfloat16)

        def far_mode(b, carry):
            lats = pl.ds(pl.multiple_of(b * columns, columns), columns)
            summed = product(updated_far[...], polynomial_rows[:, lats])
            long_out[c, b] = summed.astype(jnp.bfloat16).reshape(half, rows, columns)
            return carry

        lax.fori_loop(0, modes, far_mode, 0)
        send_long(c)

    def near_part(c):
        for first in range(0, packed, stretch):
            cut = slice(first, first + stretch)
            near = arrived[c, pl.ds(near_base, half), :, cut]
            doubled = product(doubling, near.reshape(half_radii, stretch))
            chosen = jnp.where(parity == 0, live[0][:, cut], live[1][:, cut])
            updated[:, cut] = (doubled * chosen).astype(jnp.bfloat16)

        def near_mode(kb, carry):
            b = lax.rem(my_mode + kb, modes)
            lats = pl.ds(pl.multiple_of(b * columns, columns), columns)
            summed = product(updated[...], polynomial_rows[:, lats])
            block = (c * modes + kb) * half
            held[pl.ds(block, half)] = summed.reshape(half, rows, 2, columns).astype(jnp.bfloat16)
            target = o_ref.at[c * devices + me]
            for k in range(1, half):
                i = lax.rem(my_rad + k, half)
                remote(held.at[block + i], target, out_send, out_recv, near_base + i, b).start()
            source = held.at[block + my_rad - near_base]

            @pl.when(kb > 0)
            def _():
                remote(source, target, out_send, out_recv, my_rad, b).start()

            @pl.when(kb == 0)
            def _():
                pltpu.make_async_copy(source, target, out_local).start()

            return carry

        lax.fori_loop(0, modes, near_mode, 0)

    piece = unit_room // PIECES
    short_piece = block_room // PIECES
    ahead = (packed_in.shape[1] - unit_room) // 2

    def gather():
        pltpu.make_async_copy(table_in, table_in, table_recv).wait()
        to_scalars = pltpu.make_async_copy(table_in, table, table_sem)
        to_scalars.start()
        to_scalars.wait()

        @pl.when(is_gate)
        def _():
            shape = order_out.shape[1:]
            index = BLOCK * lax.broadcasted_iota(jnp.int32, shape, 0) + lax.broadcasted_iota(
                jnp.int32, shape, 1
            )
            unit_source = jnp.zeros(shape, jnp.int32)
            block_source = jnp.zeros(shape, jnp.int32)
            unit_offset, block_offset = jnp.int32(0), jnp.int32(0)
            for group in range(group_count):
                count, first, units, first_unit = extent(near_base * modes + group)
                inside = (index >= unit_offset) & (index < unit_offset + units)
                shift = group * window_units + first_unit - unit_offset
                unit_source = jnp.where(inside, index + shift, unit_source)
                inside = (index >= block_offset) & (index < block_offset + count)
                shift = group * window_blocks + first - block_offset
                block_source = jnp.where(inside, index + shift, block_source)
                unit_offset = unit_offset + units
                block_offset = block_offset + count
            order_out[0] = unit_source
            order_out[1] = block_source
            to_scalars = pltpu.make_async_copy(order_out, order_in, table_sem)
            to_scalars.start()
            pltpu.make_async_copy(pooled, pooled, pool_recv).wait()
            to_scalars.wait()

            def one_unit(j, carry):
                source = order_in[0, j // BLOCK, lax.rem(j, BLOCK)]
                group = jnp.clip(source // window_units, 0, group_count - 1)
                unit = jnp.clip(source - group * window_units, 0, window_units - 1)
                packed_out[j] = pooled[group, unit]
                return carry

            def pack(p, carry):
                lax.fori_loop(p * piece, (p + 1) * piece, one_unit, 0)
                remote(
                    packed_out.at[pl.ds(p * piece, piece)],
                    packed_in.at[place, pl.ds(ahead + p * piece, piece)],
                    pack_send,
                    pack_recv.at[place, p],
                    far_gate_base + place,
                    my_mode,
                ).start()
                return carry

            lax.fori_loop(0, PIECES, pack, 0)

    def gather_short():
        pltpu.make_async_copy(short_pooled, short_pooled, short_pool_recv).wait()

        def one_block(j, carry):
            source = order_in[1, j // BLOCK, lax.rem(j, BLOCK)]
            group = jnp.clip(source // window_blocks, 0, group_count - 1)
            block = jnp.clip(source - group * window_blocks, 0, window_blocks - 1)
            short_packed_out[j] = short_pooled[group, block]
            return carry

        def pack(p, carry):
            lax.fori_loop(p * short_piece, (p + 1) * short_piece, one_block, 0)
            some = pl.ds(p * short_piece, short_piece)
            remote(
                short_packed_out.at[some],
                short_packed_in.at[lax.rem(my_mode, shares), some],
                short_pack_send,
                short_pack_recv.at[lax.rem(my_mode, shares), p],
                far_base + my_mode // shares * across + place,
                my_mode,
            ).start()
            return carry

        lax.fori_loop(0, PIECES, pack, 0)

    blank = jnp.zeros((ahead, UNIT, width), jnp.bfloat16)
    for y in range(across):
        packed_in[y, :ahead] = blank
        packed_in[y, ahead + unit_room :] = blank

    lax.fori_loop(0, parts, one_part, 0)

    def arrived_piece(y, p):
        some = packed_in.at[y, pl.ds(ahead + p * piece, piece)]
        return pltpu.make_async_copy(some, some, pack_recv.at[y, p])

    def relay(p, carry):
        arrived_piece(place, p).wait()
        some = packed_in.at[place, pl.ds(ahead + p * piece, piece)]

        @pl.when(is_gate)
        def _():
            remote(
                some, some, relay_send, pack_recv.at[place, p], outer_base + place, my_mode
            ).start()

        for k in range(1, across):
            remote(
                some,
                some,
                relay_send,
                pack_recv.at[place, p],
                plane_base + lax.rem(place + k, across),
                my_mode,
            ).start()
        return carry

    def short_piece_of(share, p):
        some = short_packed_in.at[share, pl.ds(p * short_piece, short_piece)]
        return pltpu.make_async_copy(some, some, short_pack_recv.at[share, p])

    my_share = lax.rem(my_mode, shares)
    is_spreader = my_mode // shares == (my_rad - near_base) // across

    def spread(p, carry):
        short_piece_of(my_share, p).wait()
        some = short_packed_in.at[my_share, pl.ds(p * short_piece, short_piece)]
        arrival = short_pack_recv.at[my_share, p]

        @pl.when(is_spreader)
        def _():
            for k in range(shares, modes, shares):
                mate = lax.rem(my_mode + k, modes)
                remote(some, some, spread_send, arrival, my_rad, mate).start()

        for k in range(1, shares):
            sibling = my_mode - my_share + lax.rem(my_share + k, shares)
            remote(some, some, spread_send, arrival, my_rad, sibling).start()
        return carry

    def late_part(c, carry):
        @pl.when(c >= EARLY)
        def _():
            far_part(c)

        @pl.when(jnp.logical_not(is_gate))
        def _():
            near_part(c)

        @pl.when((c == SHORT_AFTER) & is_gate)
        def _():
            lax.fori_loop(0, PIECES // 2, relay, 0)
            gather_short()
            lax.fori_loop(PIECES // 2, PIECES, relay, 0)

        return carry

    lax.fori_loop(0, parts, late_part, 0)

    @pl.when(jnp.logical_not(is_gate))
    def _():
        lax.fori_loop(0, PIECES, relay, 0)

    lax.fori_loop(0, PIECES, spread, 0)

    other_blocks = held.at[pl.ds(0, parts * (group_count - 1))]
    pltpu.make_async_copy(other_blocks, other_blocks, out_send).wait()
    own = pl.ds(0, parts)
    pltpu.make_async_copy(held.at[own], o_ref.at[own], out_local).wait()

    def arrived_pieces(p, carry):
        for k in range(1, across):
            arrived_piece(lax.rem(place + k, across), p).wait()
        return carry

    lax.fori_loop(0, PIECES, arrived_pieces, 0)

    def arrived_shorts(p, carry):
        for k in range(1, shares):
            short_piece_of(lax.rem(my_mode + k, shares), p).wait()

        return carry

    lax.fori_loop(0, PIECES, arrived_shorts, 0)

    sent_parts = outgoing.at[:, pl.ds(0, rads - 1)]

    pltpu.make_async_copy(sent_parts, sent_parts, in_send).wait()
    counts = [table[far_base * modes + group, 0, 0] for group in range(group_count)]
    units_of = [table[far_base * modes + group, 0, 2] for group in range(group_count)]

    def one_group(group, carry):
        count, first, _, first_unit = extent(far_base * modes + group)
        offset, unit_offset = jnp.int32(0), jnp.int32(0)
        for k in range(group_count - 1):
            offset = offset + jnp.where(k < group, counts[k], 0)
            unit_offset = unit_offset + jnp.where(k < group, units_of[k], 0)
        factors = []
        for share in range(shares):
            taken = []
            for w in range(window_blocks):
                j = jnp.clip(offset + w - first, 0, block_room - 1)
                block = short_packed_in[share, j].reshape(share_parts * rows, BLOCK)
                valid = (w >= first) & (w < first + count)
                taken.append(jnp.where(valid, block, jnp.zeros_like(block)))
            factors.append(jnp.concatenate(taken, axis=1))
        factors = jnp.concatenate(factors, axis=0)
        begin = jnp.clip(ahead + unit_offset - first_unit, 0, ahead + unit_room)
        for y in range(across):
            taken = [packed_in[y, begin + k] for k in range(window_units)]
            summed = product(factors, jnp.concatenate(taken, axis=0))
            lats = pl.ds(
                pl.multiple_of((group // rads) * columns + y * width, width), width
            )
            outgoing[:, lax.rem(group, rads), :, lats] = summed.reshape(parts, rows, width).astype(
                jnp.bfloat16
            )
        return carry

    lax.fori_loop(0, group_count, one_group, 0)

    together = modes
    size = 2 * together * rows
    row = lax.broadcasted_iota(jnp.int32, (size, size), 0)
    column = lax.broadcasted_iota(jnp.int32, (size, size), 1)
    origin = (row % 2) * (together * rows) + (row // (2 * rows)) * rows + (row % (2 * rows)) // 2
    merging = jnp.where(column == origin, 1.0, 0.0).astype(jnp.bfloat16)

    def merge_part(c, carry):
        def merge_some(q, carry):
            row_groups = long_in.at[c, pl.ds(q * together, together)]
            pltpu.make_async_copy(row_groups, row_groups, long_recv.at[c, q]).wait()
            for y in range(across):
                lats = slice(y * width, (y + 1) * width)
                leading, trailing = [], []
                for k in range(together):
                    group = q * together + k
                    taken = pl.ds(
                        pl.multiple_of((group // rads) * columns + y * width, width), width
                    )
                    from_short = outgoing[c, lax.rem(group, rads), :, taken]
                    from_long = long_in[c, group, :, lats]
                    short_first = table[far_base * modes + group, 0, 1] == 0
                    leading.append(jnp.where(short_first, from_short, from_long))
                    trailing.append(jnp.where(short_first, from_long, from_short))
                merged = product(merging, jnp.concatenate(leading + trailing, axis=0))
                block = pl.ds(c * group_count + q * together, together)
                held[block, :, :, lats] = merged.reshape(together, rows, 2, width).astype(
                    jnp.bfloat16
                )
            pltpu.make_async_copy(
                held.at[pl.ds(c * group_count + q * together, together)],
                o_ref.at[pl.ds(c * devices + far_base * modes + q * together, together)],
                far_local,
            ).start()
            return carry

        lax.fori_loop(0, group_count // together, merge_some, 0)
        return carry

    lax.fori_loop(0, parts, merge_part, 0)

    overfull = jnp.int32(0)
    for begin in (0, group_count):
        blocks_used, units_used = jnp.int32(0), jnp.int32(0)
        for group in range(begin, begin + group_count):
            blocks_used = blocks_used + table[group, 0, 0]
            units_used = units_used + table[group, 0, 2]
        overfull = jnp.where((blocks_used > block_room) | (units_used > unit_room), 1, overfull)
    flag_ref[0, 0] = overfull

    sent = table_in.at[pl.ds(0, devices - 1)]
    pltpu.make_async_copy(sent, sent, table_send).wait()
    sent = staged.at[pl.ds(0, modes * across - 1)]
    pltpu.make_async_copy(sent, sent, stage_send).wait()
    for share in range(shares):
        for i in range(half):
            sent = short_out.at[i, share]
            local = is_gate & (i % across == place) & (i // across * shares + share == my_mode)

            @pl.when(jnp.logical_not(local))
            def _():
                pltpu.make_async_copy(sent, sent, short_send).wait()

    for k in range(1, shares):
        pltpu.make_async_copy(short_packed_out, short_packed_out, spread_send).wait()

    @pl.when(is_spreader)
    def _():
        for k in range(shares, modes, shares):
            pltpu.make_async_copy(short_packed_out, short_packed_out, spread_send).wait()

    pltpu.make_async_copy(long_out, long_out, long_send).wait()

    @pl.when(is_gate)
    def _():
        pltpu.make_async_copy(packed_out, packed_out, pack_send).wait()
        pltpu.make_async_copy(packed_out, packed_out, relay_send).wait()
        pltpu.make_async_copy(short_packed_out, short_packed_out, short_pack_send).wait()

    @pl.when(jnp.logical_not(is_gate))
    def _():
        pltpu.make_async_copy(staged.at[0], staged.at[0], stage_send).wait()

    for k in range(1, across):
        pltpu.make_async_copy(packed_out, packed_out, relay_send).wait()
    remote_blocks = o_ref.at[pl.ds(0, parts * (group_count - 1))]
    pltpu.make_async_copy(remote_blocks, remote_blocks, out_recv).wait()
    far_blocks = pl.ds(0, parts * group_count)
    pltpu.make_async_copy(held.at[far_blocks], o_ref.at[far_blocks], far_local).wait()


def factored(rads, modes, unit_room, block_room, arguments):
    (
        coefficients,
        legendre,
        radial_left_factor,
        radial_right,
        eigen_rates,
        diffusivity,
        slot_order,
        slot_start,
    ) = arguments
    packed, lats = legendre.shape[2:]
    radii = radial_right.shape[1]
    fields, parts_count = coefficients.shape[:2]
    parts = fields * parts_count
    devices = rads * modes
    rows, columns = radii // rads, lats // modes
    half, across = rads // 2, rads // PLANES
    groups, width = half * modes, columns // across
    window = packed // BLOCK // 2 * BLOCK
    shares = 2 * modes // PLANES
    smem = pl.BlockSpec(memory_space=pltpu.SMEM)
    hbm = pl.BlockSpec(memory_space=pltpu.HBM)
    kept = jnp.bfloat16
    dma = pltpu.SemaphoreType.DMA
    return pl.pallas_call(
        functools.partial(factored_kernel, rads, modes, parts_count, unit_room, block_room),
        out_shape=(
            pltpu.VMEM((parts * devices, rows, 2, columns), kept),
            jax.ShapeDtypeStruct((1, 1), jnp.int32),
        ),
        in_specs=[hbm] * 8,
        out_specs=(pl.BlockSpec(memory_space=pl.ANY), smem),
        scratch_shapes=[
            pltpu.SMEM(slot_order.shape, jnp.int32),
            pltpu.SMEM(slot_start.shape, jnp.int32),
            pltpu.SMEM(diffusivity.shape, jnp.float32),
            pltpu.VMEM(eigen_rates.shape, jnp.float32),
            pltpu.VMEM(radial_left_factor.shape, jnp.float32),
            pltpu.VMEM(radial_right.shape, jnp.float32),
            pltpu.VMEM((min(3, parts), rows, rads, packed), kept),
            pltpu.VMEM((parts, rads, rows, packed), kept),
            pltpu.VMEM((parts, rads, rows, packed), kept),
            pltpu.VMEM((packed, lats), kept),
            pltpu.VMEM((radii, packed), kept),
            pltpu.VMEM((radii // 2, packed), kept),
            pltpu.VMEM((parts * groups, rows, 2, columns), kept),
            pltpu.VMEM((parts, modes, half, rows, columns), kept),
            pltpu.VMEM((parts, groups, rows, columns), kept),
            pltpu.VMEM((half, shares, window // BLOCK, parts // shares, rows, BLOCK), kept),
            pltpu.VMEM((groups, window // BLOCK, parts // shares, rows, BLOCK), kept),
            pltpu.VMEM((block_room, parts // shares, rows, BLOCK), kept),
            pltpu.VMEM((shares, block_room, parts // shares, rows, BLOCK), kept),
            pltpu.VMEM((modes * across, window // UNIT, UNIT, width), kept),
            pltpu.VMEM((groups, window // UNIT, UNIT, width), kept),
            pltpu.VMEM((unit_room, UNIT, width), kept),
            pltpu.VMEM((across, unit_room + 2 * window // UNIT, UNIT, width), kept),
            pltpu.VMEM((8, 128), jnp.int32),
            pltpu.VMEM((devices, 8, 128), jnp.int32),
            pltpu.SMEM((devices, 8, 128), jnp.int32),
            pltpu.VMEM((2, 8, 128), jnp.int32),
            pltpu.SMEM((2, 8, 128), jnp.int32),
            dma((min(3, parts),)),
            dma,
            dma((parts,)),
            dma((2,)),
            dma,
            dma,
            dma,
            dma,
            dma,
            dma,
            dma,
            dma((across, PIECES)),
            dma,
            dma,
            dma,
            dma,
            dma((shares, PIECES)),
            dma,
            dma,
            dma((parts, half)),
            dma,
            dma,
            dma,
            dma,
            dma((4,)),
        ],
        compiler_params=pltpu.CompilerParams(
            collective_id=1, has_side_effects=True, vmem_limit_bytes=50 * 2**20
        ),
    )(
        slot_order,
        slot_start,
        diffusivity,
        eigen_rates,
        radial_left_factor,
        radial_right,
        coefficients.reshape(parts, rows, rads, packed),
        legendre.reshape(packed, lats),
    )


def dense(
    rads,
    modes,
    arguments,
):
    (
        coefficients,
        legendre,
        radial_left_factor,
        radial_right,
        eigen_rates,
        diffusivity,
        slot_order,
        slot_start,
    ) = arguments
    packed, lats = legendre.shape[2:]
    radii = radial_right.shape[1]
    fields, parts_count = coefficients.shape[:2]
    parts = fields * parts_count
    devices = rads * modes
    rows, columns = radii // rads, lats // modes
    smem = pl.BlockSpec(memory_space=pltpu.SMEM)
    vmem = pl.BlockSpec(memory_space=pltpu.VMEM)
    hbm = pl.BlockSpec(memory_space=pltpu.HBM)
    return pl.pallas_call(
        functools.partial(whole_kernel, rads, modes, parts_count),
        out_shape=pltpu.VMEM((parts * devices, rows, 2, columns), jnp.bfloat16),
        in_specs=[smem, smem, smem, vmem, hbm, hbm, hbm, hbm],
        out_specs=pl.BlockSpec(memory_space=pl.ANY),
        scratch_shapes=[
            pltpu.VMEM(radial_left_factor.shape, jnp.float32),
            pltpu.VMEM(radial_right.shape, jnp.float32),
            pltpu.VMEM((parts, rows, rads, packed), jnp.bfloat16),
            pltpu.VMEM((parts, rads, rows, packed), jnp.bfloat16),
            pltpu.VMEM((parts, rads, rows, packed), jnp.bfloat16),
            pltpu.VMEM((packed, lats), jnp.bfloat16),
            pltpu.VMEM((2 * radii, packed), jnp.bfloat16),
            pltpu.VMEM((parts * devices, rows, 2, columns), jnp.bfloat16),
            pltpu.SemaphoreType.DMA((parts,)),
            pltpu.SemaphoreType.DMA,
            pltpu.SemaphoreType.DMA((parts,)),
            pltpu.SemaphoreType.DMA((2,)),
            pltpu.SemaphoreType.DMA,
            pltpu.SemaphoreType.DMA,
            pltpu.SemaphoreType.DMA,
            pltpu.SemaphoreType.DMA,
        ],
        compiler_params=pltpu.CompilerParams(
            collective_id=0, has_side_effects=True, vmem_limit_bytes=46 * 2**20
        ),
    )(
        slot_order,
        slot_start,
        diffusivity,
        eigen_rates,
        radial_left_factor,
        radial_right,
        coefficients.reshape(parts, rows, rads, packed),
        legendre.reshape(packed, lats),
    )


def on_device(rads, modes, *arguments):
    coefficients, legendre, _, radial_right = arguments[:4]
    packed, lats = legendre.shape[2:]
    rows, columns = radial_right.shape[1] // rads, lats // modes
    fields, parts_count = coefficients.shape[:2]
    parts = fields * parts_count
    half, across = rads // 2, rads // PLANES
    groups = half * modes
    window_blocks = packed // BLOCK // 2
    window_units = window_blocks * BLOCK // UNIT
    block_room = 3 * groups * window_blocks // 4
    unit_room = 21 * groups * window_units // 32
    shares = 2 * modes // PLANES
    fits = (
        rads % PLANES == 0
        and 2 * modes % PLANES == 0
        and parts % max(shares, 1) == 0
        and columns % (BLOCK * across) == 0
        and groups <= rads * (packed // columns)
        and unit_room % PIECES == 0
        and unit_room <= 8 * BLOCK
        and across * unit_room * UNIT * (columns // across) <= 2**22
    )
    if fits:
        landed, flag = factored(rads, modes, unit_room, block_room, arguments)
        landed = lax.switch(
            flag[0, 0], (lambda: landed, lambda: dense(rads, modes, arguments))
        )
    else:
        landed = dense(rads, modes, arguments)
    return landed.reshape(fields, parts_count, rads, modes, rows, 2, columns)


def solution(mesh):
    rads, modes = mesh.shape["rad"], mesh.shape["mode"]
    return jax.shard_map(
        functools.partial(on_device, rads, modes),
        mesh=mesh,
        in_specs=(
            P(None, None, "rad", None, "mode", None),
            P("rad", "mode", None, None),
            P(),
            P(),
            P(),
            P(),
            P("rad", "mode", None),
            P("rad", "mode", None),
        ),
        out_specs=P(None, None, None, None, "rad", None, "mode"),
        check_vma=False,
    )
```

```python
import functools
import jax
import jax.numpy as jnp
from jax import lax
from jax.experimental import pallas as pl
from jax.experimental.pallas import tpu as pltpu
from jax.sharding import PartitionSpec as P

DEGREES = 1024
BLOCK = 128
MESH = pl.DeviceIdType.MESH


def far_first(count):
    return sorted(range(count), key=lambda k: (-min(k, count - k), k))


def whole_kernel(
    rads,
    modes,
    parts_count,
    order_ref,
    start_ref,
    diffusivity_ref,
    eigen_ref,
    left_hbm,
    right_hbm,
    x_ref,
    legendre_ref,
    o_ref,
    left_ref,
    right_ref,
    entering,
    outgoing,
    arrived,
    polynomial_rows,
    updated,
    held,
    enter_sem,
    in_send,
    in_recv,
    factor_sem,
    legendre_sem,
    out_send,
    out_recv,
    out_local,
):
    my_rad = lax.axis_index("rad")
    my_mode = lax.axis_index("mode")
    devices = rads * modes
    parts = arrived.shape[0]
    packed = arrived.shape[3]
    radii = right_ref.shape[1]
    rows, lats = held.shape[1], held.shape[3]
    me = my_rad * modes + my_mode

    def enter(c):
        return pltpu.make_async_copy(x_ref.at[c], entering.at[c], enter_sem.at[c])

    for c in range(parts):
        enter(c).start()
    fetches = (
        pltpu.make_async_copy(left_hbm, left_ref, factor_sem.at[0]),
        pltpu.make_async_copy(right_hbm, right_ref, factor_sem.at[1]),
        pltpu.make_async_copy(legendre_ref, polynomial_rows, legendre_sem),
    )
    for fetch in fetches:
        fetch.start()
    barrier = pltpu.get_barrier_semaphore()
    for ka in range(rads):
        for kb in range(modes):
            if ka or kb:
                peer = (lax.rem(my_rad + ka, rads), lax.rem(my_mode + kb, modes))
                pl.semaphore_signal(barrier, inc=1, device_id=peer, device_id_type=MESH)

    def turn(c):
        enter(c).wait()
        outgoing[c] = jnp.swapaxes(entering[c], 0, 1)

    turn(0)
    pl.semaphore_wait(barrier, devices - 1)

    def send_part(c, carry):
        @pl.when(c > 0)
        def _():
            turn(c)

        for ka in far_first(rads):
            a = lax.rem(my_rad + ka, rads)
            source = outgoing.at[c, a]
            target = arrived.at[c, my_rad]
            if ka:
                pltpu.make_async_remote_copy(
                    src_ref=source,
                    dst_ref=target,
                    send_sem=in_send,
                    recv_sem=in_recv.at[c],
                    device_id=(a, my_mode),
                    device_id_type=MESH,
                ).start()
            else:
                pltpu.make_async_copy(source, target, in_recv.at[c]).start()
        return carry

    lax.fori_loop(0, parts, send_part, 0)

    position = lax.broadcasted_iota(jnp.int32, (1, packed), 1)
    live = []
    degree = jnp.zeros((1, packed), jnp.int32)
    for s in range(2):
        order = order_ref[0, 0, s]
        start = start_ref[0, 0, s]
        first_degree = BLOCK * (order // BLOCK)
        inside = (position >= start) & (position < start + DEGREES - first_degree)
        row_degree = first_degree + position - start
        degree = degree + jnp.where(inside, row_degree, 0)
        live.append(jnp.where(inside & (row_degree >= order), 1.0, 0.0).astype(jnp.float32))
    degree_level = degree.astype(jnp.float32)
    harmonic = degree_level * (degree_level + 1.0) / (DEGREES * DEGREES)
    covered = jnp.maximum(live[0], live[1])
    row = lax.broadcasted_iota(jnp.int32, (2 * radii, radii), 0)
    column = lax.broadcasted_iota(jnp.int32, (2 * radii, radii), 1)
    doubling = jnp.where(row // 2 == column, 1.0, 0.0).astype(jnp.bfloat16)
    parity = lax.broadcasted_iota(jnp.int32, (2 * radii, packed), 0) % 2
    for fetch in fetches:
        fetch.wait()

    def one_part(c, carry):
        field = c // parts_count
        pltpu.make_async_copy(arrived.at[c], arrived.at[c], in_recv.at[c]).wait()
        rates = eigen_ref[pl.ds(field, 1), :]
        rates = jnp.transpose(jnp.broadcast_to(rates, (128, radii)))[:, 0:1]
        shrink = 1.0 + rates + diffusivity_ref[field] * harmonic
        values = arrived[c].reshape(radii, packed).astype(jnp.float32)
        turned = jnp.dot(
            left_ref[field], values, precision=lax.Precision.HIGHEST, preferred_element_type=jnp.float32
        )
        scaled = turned * (covered / shrink)
        result = jnp.dot(
            right_ref[field], scaled, precision=lax.Precision.HIGHEST, preferred_element_type=jnp.float32
        )
        doubled = jnp.dot(doubling, result.astype(jnp.bfloat16), preferred_element_type=jnp.float32)
        updated[...] = (doubled * jnp.where(parity == 0, live[0], live[1])).astype(jnp.bfloat16)
        for kb in range(modes):
            b = lax.rem(my_mode + kb, modes)
            columns = pl.ds(pl.multiple_of(b * lats, lats), lats)
            summed = jnp.dot(
                updated[...], polynomial_rows[:, columns], preferred_element_type=jnp.float32
            )
            blocks = summed.reshape(rads, rows, 2, lats).astype(jnp.bfloat16)
            for a in range(rads):
                held[(c * modes + kb) * rads + a] = blocks[a]
            for ka in far_first(rads):
                a = lax.rem(my_rad + ka, rads)
                source = held.at[(c * modes + kb) * rads + a]
                target = o_ref.at[c * devices + me]
                if ka or kb:
                    pltpu.make_async_remote_copy(
                        src_ref=source,
                        dst_ref=target,
                        send_sem=out_send,
                        recv_sem=out_recv,
                        device_id=(a, b),
                        device_id_type=MESH,
                    ).start()
                else:
                    pltpu.make_async_copy(source, target, out_local).start()
        return carry

    lax.fori_loop(0, parts, one_part, 0)
    others = arrived.at[:, pl.ds(0, rads - 1)]
    pltpu.make_async_copy(others, others, in_send).wait()
    remote = pl.ds(0, parts * (devices - 1))
    pltpu.make_async_copy(held.at[remote], held.at[remote], out_send).wait()
    pltpu.make_async_copy(o_ref.at[remote], o_ref.at[remote], out_recv).wait()
    own = pl.ds(0, parts)
    pltpu.make_async_copy(held.at[own], o_ref.at[own], out_local).wait()


PLANES = 4
EARLY = 2
SHORT_AFTER = 2
PIECES = 4
UNIT = 16


def pieces_of(value, count):
    pieces = []
    for _ in range(count):
        piece = value.astype(jnp.bfloat16)
        pieces.append(piece)
        value = value - piece.astype(jnp.float32)
    return pieces


def product(left, right):
    return jnp.dot(left, right, preferred_element_type=jnp.float32)


def factored_kernel(
    rads,
    modes,
    parts_count,
    unit_room,
    block_room,
    order_hbm,
    start_hbm,
    diffusivity_hbm,
    eigen_hbm,
    left_hbm,
    right_hbm,
    x_ref,
    legendre_ref,
    o_ref,
    flag_ref,
    order_ref,
    start_ref,
    diffusivity_ref,
    eigen_ref,
    left_ref,
    right_ref,
    entering,
    outgoing,
    arrived,
    polynomial_rows,
    updated,
    updated_far,
    held,
    long_out,
    long_in,
    short_out,
    short_pooled,
    short_packed_out,
    short_packed_in,
    staged,
    pooled,
    packed_out,
    packed_in,
    table_out,
    table_in,
    table,
    order_out,
    order_in,
    enter_sem,
    in_send,
    in_recv,
    factor_sem,
    legendre_sem,
    table_send,
    table_recv,
    table_sem,
    stage_send,
    pool_recv,
    pack_send,
    pack_recv,
    relay_send,
    short_send,
    short_pool_recv,
    short_pack_send,
    short_pack_recv,
    spread_send,
    long_send,
    long_recv,
    out_send,
    out_recv,
    out_local,
    setting_sem,
):
    my_rad = lax.axis_index("rad")
    my_mode = lax.axis_index("mode")
    devices = rads * modes
    slots = entering.shape[0]
    parts = arrived.shape[0]
    packed = arrived.shape[3]
    radii = right_ref.shape[1]
    rows, columns = held.shape[1], held.shape[3]
    half = rads // 2
    across = rads // PLANES
    group_count = half * modes
    window_units = staged.shape[1]
    window_blocks = window_units * UNIT // BLOCK
    window = window_units * UNIT
    shares = short_out.shape[1]
    share_parts = parts // shares
    width = staged.shape[3]
    me = my_rad * modes + my_mode
    side = my_rad // half
    near_base = side * half
    far_base = half - near_base
    gate_base = half - across + side * across
    far_gate_base = half - side * across
    outer_base = side * (rads - across)
    place = lax.rem(my_rad, across)
    plane_base = my_rad - place
    is_gate = plane_base == gate_base
    my_group = (my_rad - near_base) * modes + my_mode

    def remote(source, target, send_sem, recv_sem, rad, mode):
        return pltpu.make_async_remote_copy(
            src_ref=source,
            dst_ref=target,
            send_sem=send_sem,
            recv_sem=recv_sem,
            device_id=(rad, mode),
            device_id_type=MESH,
        )

    barrier = pltpu.get_barrier_semaphore()
    for ka in far_first(rads):
        for kb in far_first(modes):
            if ka or kb:
                peer = (lax.rem(my_rad + ka, rads), lax.rem(my_mode + kb, modes))
                pl.semaphore_signal(barrier, inc=1, device_id=peer, device_id_type=MESH)

    def enter(c):
        slot = lax.rem(c, slots)
        return pltpu.make_async_copy(x_ref.at[c], entering.at[slot], enter_sem.at[slot])

    settings = (
        pltpu.make_async_copy(order_hbm, order_ref, setting_sem.at[0]),
        pltpu.make_async_copy(start_hbm, start_ref, setting_sem.at[1]),
        pltpu.make_async_copy(diffusivity_hbm, diffusivity_ref, setting_sem.at[2]),
        pltpu.make_async_copy(eigen_hbm, eigen_ref, setting_sem.at[3]),
    )
    enter(0).start()
    for setting in settings:
        setting.start()
    for c in range(1, min(slots, parts)):
        enter(c).start()
    fetches = (
        pltpu.make_async_copy(left_hbm, left_ref, factor_sem.at[0]),
        pltpu.make_async_copy(right_hbm, right_ref, factor_sem.at[1]),
    )
    fetch_legendre = pltpu.make_async_copy(legendre_ref, polynomial_rows, legendre_sem)
    fetch_legendre.start()
    for fetch in fetches:
        fetch.start()

    def extent(device):
        count = table[device, 0, 0]
        short_first = table[device, 0, 1] == 0
        units = table[device, 0, 2]
        first = jnp.where(short_first, 0, window_blocks - count)
        first_unit = jnp.where(short_first, count * (BLOCK // UNIT) - units, window_units - units)
        return count, first, units, first_unit

    def turn(c):
        enter(c).wait()
        outgoing[c] = jnp.swapaxes(entering[lax.rem(c, slots)], 0, 1)

        @pl.when(c + slots < parts)
        def _():
            enter(c + slots).start()

    turn(0)
    settings[0].wait()

    blocks = [DEGREES // BLOCK - order_ref[0, 0, s] // BLOCK for s in range(2)]
    short = jnp.where(blocks[0] <= blocks[1], 0, 1)
    short_blocks = jnp.minimum(jnp.minimum(blocks[0], blocks[1]), window_blocks)
    short_order = jnp.where(short == 0, order_ref[0, 0, 0], order_ref[0, 0, 1])
    unused = (short_order - BLOCK * (short_order // BLOCK)) // UNIT
    short_units = short_blocks * (BLOCK // UNIT) - unused
    lane = lax.broadcasted_iota(jnp.int32, table_out.shape, 1)
    entries = jnp.where(lane == 2, short_units, 0)
    entries = jnp.where(lane == 1, short, entries)
    table_out[...] = jnp.where(lane == 0, short_blocks, entries)

    pl.semaphore_wait(barrier, devices - 1)

    def send_part(c, carry):
        @pl.when(c > 0)
        def _():
            turn(c)

        for k in range(half):
            a = far_base + lax.rem(my_rad + k, half)
            remote(
                outgoing.at[c, a], arrived.at[c, my_rad], in_send, in_recv.at[c], a, my_mode
            ).start()
        for k in range(1, half):
            a = near_base + lax.rem(my_rad + k, half)
            remote(
                outgoing.at[c, a], arrived.at[c, my_rad], in_send, in_recv.at[c], a, my_mode
            ).start()
        pltpu.make_async_copy(outgoing.at[c, my_rad], arrived.at[c, my_rad], in_recv.at[c]).start()
        return carry

    lax.fori_loop(0, 1, send_part, 0)
    for k in range(1, devices):
        d = lax.rem(me + k, devices)
        remote(
            table_out,
            table_in.at[me],
            table_send,
            table_recv,
            d // modes,
            lax.rem(d, modes),
        ).start()
    pltpu.make_async_copy(table_out, table_in.at[me], table_recv).start()

    lax.fori_loop(1, EARLY, send_part, 0)

    fetch_legendre.wait()
    for b in range(modes):
        for y in range(across):
            lats = slice(b * columns + y * width, b * columns + (y + 1) * width)
            leading = polynomial_rows[:window, lats]
            trailing = polynomial_rows[packed - window :, lats]
            chosen = jnp.where(short == 0, leading, trailing)
            staged[b * across + y] = chosen.reshape(window_units, UNIT, width)
    for kb in range(modes):
        b = lax.rem(my_mode + kb, modes)
        for ky in range(across):
            y = lax.rem(place + ky, across)
            source = staged.at[b * across + y]
            target = pooled.at[my_group]
            if kb or ky:
                remote(source, target, stage_send, pool_recv, gate_base + y, b).start()
            else:

                @pl.when(is_gate)
                def _():
                    pltpu.make_async_copy(source, target, pool_recv).start()

                @pl.when(jnp.logical_not(is_gate))
                def _():
                    remote(source, target, stage_send, pool_recv, gate_base + y, b).start()

    lax.fori_loop(EARLY, parts, send_part, 0)

    for setting in settings[1:]:
        setting.wait()
    position = lax.broadcasted_iota(jnp.int32, (1, packed), 1)
    live = []
    degree = jnp.zeros((1, packed), jnp.int32)
    for s in range(2):
        order = order_ref[0, 0, s]
        start = start_ref[0, 0, s]
        first_degree = BLOCK * (order // BLOCK)
        inside = (position >= start) & (position < start + DEGREES - first_degree)
        row_degree = first_degree + position - start
        degree = degree + jnp.where(inside, row_degree, 0)
        live.append(jnp.where(inside & (row_degree >= order), 1.0, 0.0).astype(jnp.float32))
    degree_level = degree.astype(jnp.float32)
    harmonic = degree_level * (degree_level + 1.0) / (DEGREES * DEGREES)
    covered = jnp.maximum(live[0], live[1])
    live_short = jnp.where(short == 0, live[0], live[1])
    live_long = jnp.where(short == 0, live[1], live[0])
    half_radii = half * rows
    row = lax.broadcasted_iota(jnp.int32, (2 * half_radii, half_radii), 0)
    column = lax.broadcasted_iota(jnp.int32, (2 * half_radii, half_radii), 1)
    doubling = jnp.where(row // 2 == column, 1.0, 0.0).astype(jnp.bfloat16)
    stretch = packed // 3 if packed % (3 * BLOCK) == 0 else packed
    parity = lax.broadcasted_iota(jnp.int32, (2 * half_radii, stretch), 0) % 2
    for fetch in fetches:
        fetch.wait()

    def send_long(c):
        for kb in range(modes):
            b = lax.rem(my_mode + kb, modes)
            for k in range(half):
                i = lax.rem(my_rad + k, half)
                remote(
                    long_out.at[c, b, i],
                    long_in.at[c, my_group],
                    long_send,
                    long_recv.at[c, my_rad - near_base],
                    far_base + i,
                    b,
                ).start()

    def one_part(c, carry):
        field = c // parts_count
        pltpu.make_async_copy(arrived.at[c], arrived.at[c], in_recv.at[c]).wait()
        rates = eigen_ref[pl.ds(field, 1), :]
        rates = jnp.transpose(jnp.broadcast_to(rates, (128, radii)))[:, 0:1]
        left = pieces_of(left_ref[field], 3)
        right = pieces_of(right_ref[field], 2)
        for first in range(0, packed, stretch):
            cut = slice(first, first + stretch)
            shrink = 1.0 + rates + diffusivity_ref[field] * harmonic[:, cut]
            values = arrived[c, :, :, cut].reshape(radii, stretch)
            turned = product(left[2], values) + product(left[1], values) + product(left[0], values)
            high, low = pieces_of(turned * (covered[:, cut] / shrink), 2)
            result = product(right[0], low) + product(right[1], high) + product(right[0], high)
            arrived[c, :, :, cut] = result.astype(jnp.bfloat16).reshape(rads, rows, stretch)

        far = arrived[c, pl.ds(far_base, half)].reshape(half_radii, packed).astype(jnp.float32)
        masked = (far * live_short).astype(jnp.bfloat16)
        masked = jnp.where(short == 0, masked[:, :window], masked[:, packed - window :])
        share, place_in_share = c // share_parts, lax.rem(c, share_parts)
        for i in range(half):
            for w in range(window_blocks):
                short_out[i, share, w, place_in_share] = masked[
                    i * rows : (i + 1) * rows, w * BLOCK : (w + 1) * BLOCK
                ]

        @pl.when(place_in_share == share_parts - 1)
        def _():
            for k in range(half):
                i = lax.rem(my_rad + k, half)
                y = lax.rem(i, across)
                b = i // across * shares + share
                source, target = short_out.at[i, share], short_pooled.at[my_group]
                local = is_gate & (y == place) & (b == my_mode)

                @pl.when(local)
                def _():
                    pltpu.make_async_copy(source, target, short_pool_recv).start()

                @pl.when(jnp.logical_not(local))
                def _():
                    remote(source, target, short_send, short_pool_recv, gate_base + y, b).start()

        @pl.when(c < EARLY)
        def _():
            far_part(c)

        @pl.when(is_gate)
        def _():
            near_part(c)

        @pl.when(c == EARLY - 1)
        def _():
            gather()

        return carry

    def far_part(c):
        far = arrived[c, pl.ds(far_base, half)].reshape(half_radii, packed).astype(jnp.float32)
        updated_far[...] = (far * live_long).astype(jnp.bfloat16)

        def far_mode(b, carry):
            lats = pl.ds(pl.multiple_of(b * columns, columns), columns)
            summed = product(updated_far[...], polynomial_rows[:, lats])
            long_out[c, b] = summed.astype(jnp.bfloat16).reshape(half, rows, columns)
            return carry

        lax.fori_loop(0, modes, far_mode, 0)
        send_long(c)

    def near_part(c):
        for first in range(0, packed, stretch):
            cut = slice(first, first + stretch)
            near = arrived[c, pl.ds(near_base, half), :, cut]
            doubled = product(doubling, near.reshape(half_radii, stretch))
            chosen = jnp.where(parity == 0, live[0][:, cut], live[1][:, cut])
            updated[:, cut] = (doubled * chosen).astype(jnp.bfloat16)

        def near_mode(kb, carry):
            b = lax.rem(my_mode + kb, modes)
            lats = pl.ds(pl.multiple_of(b * columns, columns), columns)
            summed = product(updated[...], polynomial_rows[:, lats])
            block = (c * modes + kb) * half
            held[pl.ds(block, half)] = summed.reshape(half, rows, 2, columns).astype(jnp.bfloat16)
            target = o_ref.at[c * devices + me]
            for k in range(1, half):
                i = lax.rem(my_rad + k, half)
                remote(held.at[block + i], target, out_send, out_recv, near_base + i, b).start()
            source = held.at[block + my_rad - near_base]

            @pl.when(kb > 0)
            def _():
                remote(source, target, out_send, out_recv, my_rad, b).start()

            @pl.when(kb == 0)
            def _():
                pltpu.make_async_copy(source, target, out_local).start()

            return carry

        lax.fori_loop(0, modes, near_mode, 0)

    piece = unit_room // PIECES
    short_piece = block_room // PIECES
    ahead = (packed_in.shape[1] - unit_room) // 2

    def gather():
        pltpu.make_async_copy(table_in, table_in, table_recv).wait()
        to_scalars = pltpu.make_async_copy(table_in, table, table_sem)
        to_scalars.start()
        to_scalars.wait()

        @pl.when(is_gate)
        def _():
            shape = order_out.shape[1:]
            index = BLOCK * lax.broadcasted_iota(jnp.int32, shape, 0) + lax.broadcasted_iota(
                jnp.int32, shape, 1
            )
            unit_source = jnp.zeros(shape, jnp.int32)
            block_source = jnp.zeros(shape, jnp.int32)
            unit_offset, block_offset = jnp.int32(0), jnp.int32(0)
            for group in range(group_count):
                count, first, units, first_unit = extent(near_base * modes + group)
                inside = (index >= unit_offset) & (index < unit_offset + units)
                shift = group * window_units + first_unit - unit_offset
                unit_source = jnp.where(inside, index + shift, unit_source)
                inside = (index >= block_offset) & (index < block_offset + count)
                shift = group * window_blocks + first - block_offset
                block_source = jnp.where(inside, index + shift, block_source)
                unit_offset = unit_offset + units
                block_offset = block_offset + count
            order_out[0] = unit_source
            order_out[1] = block_source
            to_scalars = pltpu.make_async_copy(order_out, order_in, table_sem)
            to_scalars.start()
            pltpu.make_async_copy(pooled, pooled, pool_recv).wait()
            to_scalars.wait()

            def one_unit(j, carry):
                source = order_in[0, j // BLOCK, lax.rem(j, BLOCK)]
                group = jnp.clip(source // window_units, 0, group_count - 1)
                unit = jnp.clip(source - group * window_units, 0, window_units - 1)
                packed_out[j] = pooled[group, unit]
                return carry

            def pack(p, carry):
                lax.fori_loop(p * piece, (p + 1) * piece, one_unit, 0)
                remote(
                    packed_out.at[pl.ds(p * piece, piece)],
                    packed_in.at[place, pl.ds(ahead + p * piece, piece)],
                    pack_send,
                    pack_recv.at[place, p],
                    far_gate_base + place,
                    my_mode,
                ).start()
                return carry

            lax.fori_loop(0, PIECES, pack, 0)

    def gather_short():
        pltpu.make_async_copy(short_pooled, short_pooled, short_pool_recv).wait()

        def one_block(j, carry):
            source = order_in[1, j // BLOCK, lax.rem(j, BLOCK)]
            group = jnp.clip(source // window_blocks, 0, group_count - 1)
            block = jnp.clip(source - group * window_blocks, 0, window_blocks - 1)
            short_packed_out[j] = short_pooled[group, block]
            return carry

        def pack(p, carry):
            lax.fori_loop(p * short_piece, (p + 1) * short_piece, one_block, 0)
            some = pl.ds(p * short_piece, short_piece)
            remote(
                short_packed_out.at[some],
                short_packed_in.at[lax.rem(my_mode, shares), some],
                short_pack_send,
                short_pack_recv.at[lax.rem(my_mode, shares), p],
                far_base + my_mode // shares * across + place,
                my_mode,
            ).start()
            return carry

        lax.fori_loop(0, PIECES, pack, 0)

    blank = jnp.zeros((ahead, UNIT, width), jnp.bfloat16)
    for y in range(across):
        packed_in[y, :ahead] = blank
        packed_in[y, ahead + unit_room :] = blank

    lax.fori_loop(0, parts, one_part, 0)

    def arrived_piece(y, p):
        some = packed_in.at[y, pl.ds(ahead + p * piece, piece)]
        return pltpu.make_async_copy(some, some, pack_recv.at[y, p])

    def relay(p, carry):
        arrived_piece(place, p).wait()
        some = packed_in.at[place, pl.ds(ahead + p * piece, piece)]

        @pl.when(is_gate)
        def _():
            remote(
                some, some, relay_send, pack_recv.at[place, p], outer_base + place, my_mode
            ).start()

        for k in range(1, across):
            remote(
                some,
                some,
                relay_send,
                pack_recv.at[place, p],
                plane_base + lax.rem(place + k, across),
                my_mode,
            ).start()
        return carry

    def short_piece_of(share, p):
        some = short_packed_in.at[share, pl.ds(p * short_piece, short_piece)]
        return pltpu.make_async_copy(some, some, short_pack_recv.at[share, p])

    my_share = lax.rem(my_mode, shares)
    is_spreader = my_mode // shares == (my_rad - near_base) // across

    def spread(p, carry):
        short_piece_of(my_share, p).wait()
        some = short_packed_in.at[my_share, pl.ds(p * short_piece, short_piece)]
        arrival = short_pack_recv.at[my_share, p]

        @pl.when(is_spreader)
        def _():
            for k in range(shares, modes, shares):
                mate = lax.rem(my_mode + k, modes)
                remote(some, some, spread_send, arrival, my_rad, mate).start()

        for k in range(1, shares):
            sibling = my_mode - my_share + lax.rem(my_share + k, shares)
            remote(some, some, spread_send, arrival, my_rad, sibling).start()
        return carry

    def late_part(c, carry):
        @pl.when(c >= EARLY)
        def _():
            far_part(c)

        @pl.when(jnp.logical_not(is_gate))
        def _():
            near_part(c)

        @pl.when((c == SHORT_AFTER) & is_gate)
        def _():
            lax.fori_loop(0, PIECES // 2, relay, 0)
            gather_short()
            lax.fori_loop(PIECES // 2, PIECES, relay, 0)

        return carry

    lax.fori_loop(0, parts, late_part, 0)

    @pl.when(jnp.logical_not(is_gate))
    def _():
        lax.fori_loop(0, PIECES, relay, 0)

    lax.fori_loop(0, PIECES, spread, 0)

    other_blocks = held.at[pl.ds(0, parts * (group_count - 1))]
    pltpu.make_async_copy(other_blocks, other_blocks, out_send).wait()
    own = pl.ds(0, parts)
    pltpu.make_async_copy(held.at[own], o_ref.at[own], out_local).wait()

    def arrived_pieces(p, carry):
        for k in range(1, across):
            arrived_piece(lax.rem(place + k, across), p).wait()
        return carry

    lax.fori_loop(0, PIECES, arrived_pieces, 0)

    def arrived_shorts(p, carry):
        for k in range(1, shares):
            short_piece_of(lax.rem(my_mode + k, shares), p).wait()

        return carry

    lax.fori_loop(0, PIECES, arrived_shorts, 0)

    sent_parts = outgoing.at[:, pl.ds(0, rads - 1)]

    pltpu.make_async_copy(sent_parts, sent_parts, in_send).wait()
    counts = [table[far_base * modes + group, 0, 0] for group in range(group_count)]
    units_of = [table[far_base * modes + group, 0, 2] for group in range(group_count)]

    def one_group(group, carry):
        count, first, _, first_unit = extent(far_base * modes + group)
        offset, unit_offset = jnp.int32(0), jnp.int32(0)
        for k in range(group_count - 1):
            offset = offset + jnp.where(k < group, counts[k], 0)
            unit_offset = unit_offset + jnp.where(k < group, units_of[k], 0)
        factors = []
        for share in range(shares):
            taken = []
            for w in range(window_blocks):
                j = jnp.clip(offset + w - first, 0, block_room - 1)
                block = short_packed_in[share, j].reshape(share_parts * rows, BLOCK)
                valid = (w >= first) & (w < first + count)
                taken.append(jnp.where(valid, block, jnp.zeros_like(block)))
            factors.append(jnp.concatenate(taken, axis=1))
        factors = jnp.concatenate(factors, axis=0)
        begin = jnp.clip(ahead + unit_offset - first_unit, 0, ahead + unit_room)
        for y in range(across):
            taken = [packed_in[y, begin + k] for k in range(window_units)]
            summed = product(factors, jnp.concatenate(taken, axis=0))
            lats = pl.ds(
                pl.multiple_of((group // rads) * columns + y * width, width), width
            )
            outgoing[:, lax.rem(group, rads), :, lats] = summed.reshape(parts, rows, width).astype(
                jnp.bfloat16
            )
        return carry

    lax.fori_loop(0, group_count, one_group, 0)

    together = modes
    size = 2 * together * rows
    row = lax.broadcasted_iota(jnp.int32, (size, size), 0)
    column = lax.broadcasted_iota(jnp.int32, (size, size), 1)
    origin = (row % 2) * (together * rows) + (row // (2 * rows)) * rows + (row % (2 * rows)) // 2
    merging = jnp.where(column == origin, 1.0, 0.0).astype(jnp.bfloat16)

    def merge_part(c, carry):
        def merge_some(q, carry):
            row_groups = long_in.at[c, pl.ds(q * together, together)]
            pltpu.make_async_copy(row_groups, row_groups, long_recv.at[c, q]).wait()
            for y in range(across):
                lats = slice(y * width, (y + 1) * width)
                leading, trailing = [], []
                for k in range(together):
                    group = q * together + k
                    taken = pl.ds(
                        pl.multiple_of((group // rads) * columns + y * width, width), width
                    )
                    from_short = outgoing[c, lax.rem(group, rads), :, taken]
                    from_long = long_in[c, group, :, lats]
                    short_first = table[far_base * modes + group, 0, 1] == 0
                    leading.append(jnp.where(short_first, from_short, from_long))
                    trailing.append(jnp.where(short_first, from_long, from_short))
                merged = product(merging, jnp.concatenate(leading + trailing, axis=0))
                block = pl.ds(c * devices + far_base * modes + q * together, together)
                o_ref[block, :, :, lats] = merged.reshape(together, rows, 2, width).astype(
                    jnp.bfloat16
                )
            return carry

        lax.fori_loop(0, group_count // together, merge_some, 0)
        return carry

    lax.fori_loop(0, parts - 1, merge_part, 0)

    overfull = jnp.int32(0)
    for begin in (0, group_count):
        blocks_used, units_used = jnp.int32(0), jnp.int32(0)
        for group in range(begin, begin + group_count):
            blocks_used = blocks_used + table[group, 0, 0]
            units_used = units_used + table[group, 0, 2]
        overfull = jnp.where((blocks_used > block_room) | (units_used > unit_room), 1, overfull)
    flag_ref[0, 0] = overfull

    sent = table_in.at[pl.ds(0, devices - 1)]
    pltpu.make_async_copy(sent, sent, table_send).wait()
    sent = staged.at[pl.ds(0, modes * across - 1)]
    pltpu.make_async_copy(sent, sent, stage_send).wait()
    for share in range(shares):
        for i in range(half):
            sent = short_out.at[i, share]
            local = is_gate & (i % across == place) & (i // across * shares + share == my_mode)

            @pl.when(jnp.logical_not(local))
            def _():
                pltpu.make_async_copy(sent, sent, short_send).wait()

    for k in range(1, shares):
        pltpu.make_async_copy(short_packed_out, short_packed_out, spread_send).wait()

    @pl.when(is_spreader)
    def _():
        for k in range(shares, modes, shares):
            pltpu.make_async_copy(short_packed_out, short_packed_out, spread_send).wait()


    @pl.when(is_gate)
    def _():
        pltpu.make_async_copy(packed_out, packed_out, pack_send).wait()
        pltpu.make_async_copy(packed_out, packed_out, relay_send).wait()
        pltpu.make_async_copy(short_packed_out, short_packed_out, short_pack_send).wait()

    @pl.when(jnp.logical_not(is_gate))
    def _():
        pltpu.make_async_copy(staged.at[0], staged.at[0], stage_send).wait()

    for k in range(1, across):
        pltpu.make_async_copy(packed_out, packed_out, relay_send).wait()
    remote_blocks = o_ref.at[pl.ds(0, parts * (group_count - 1))]
    pltpu.make_async_copy(remote_blocks, remote_blocks, out_recv).wait()

    lax.fori_loop(parts - 1, parts, merge_part, 0)
    pltpu.make_async_copy(long_out, long_out, long_send).wait()


def factored(rads, modes, unit_room, block_room, arguments):
    (
        coefficients,
        legendre,
        radial_left_factor,
        radial_right,
        eigen_rates,
        diffusivity,
        slot_order,
        slot_start,
    ) = arguments
    packed, lats = legendre.shape[2:]
    radii = radial_right.shape[1]
    fields, parts_count = coefficients.shape[:2]
    parts = fields * parts_count
    devices = rads * modes
    rows, columns = radii // rads, lats // modes
    half, across = rads // 2, rads // PLANES
    groups, width = half * modes, columns // across
    window = packed // BLOCK // 2 * BLOCK
    shares = 2 * modes // PLANES
    smem = pl.BlockSpec(memory_space=pltpu.SMEM)
    hbm = pl.BlockSpec(memory_space=pltpu.HBM)
    kept = jnp.bfloat16
    dma = pltpu.SemaphoreType.DMA
    return pl.pallas_call(
        functools.partial(factored_kernel, rads, modes, parts_count, unit_room, block_room),
        out_shape=(
            pltpu.VMEM((parts * devices, rows, 2, columns), kept),
            jax.ShapeDtypeStruct((1, 1), jnp.int32),
        ),
        in_specs=[hbm] * 8,
        out_specs=(pl.BlockSpec(memory_space=pltpu.VMEM), smem),
        scratch_shapes=[
            pltpu.SMEM(slot_order.shape, jnp.int32),
            pltpu.SMEM(slot_start.shape, jnp.int32),
            pltpu.SMEM(diffusivity.shape, jnp.float32),
            pltpu.VMEM(eigen_rates.shape, jnp.float32),
            pltpu.VMEM(radial_left_factor.shape, jnp.float32),
            pltpu.VMEM(radial_right.shape, jnp.float32),
            pltpu.VMEM((min(3, parts), rows, rads, packed), kept),
            pltpu.VMEM((parts, rads, rows, packed), kept),
            pltpu.VMEM((parts, rads, rows, packed), kept),
            pltpu.VMEM((packed, lats), kept),
            pltpu.VMEM((radii, packed), kept),
            pltpu.VMEM((radii // 2, packed), kept),
            pltpu.VMEM((parts * groups, rows, 2, columns), kept),
            pltpu.VMEM((parts, modes, half, rows, columns), kept),
            pltpu.VMEM((parts, groups, rows, columns), kept),
            pltpu.VMEM((half, shares, window // BLOCK, parts // shares, rows, BLOCK), kept),
            pltpu.VMEM((groups, window // BLOCK, parts // shares, rows, BLOCK), kept),
            pltpu.VMEM((block_room, parts // shares, rows, BLOCK), kept),
            pltpu.VMEM((shares, block_room, parts // shares, rows, BLOCK), kept),
            pltpu.VMEM((modes * across, window // UNIT, UNIT, width), kept),
            pltpu.VMEM((groups, window // UNIT, UNIT, width), kept),
            pltpu.VMEM((unit_room, UNIT, width), kept),
            pltpu.VMEM((across, unit_room + 2 * window // UNIT, UNIT, width), kept),
            pltpu.VMEM((8, 128), jnp.int32),
            pltpu.VMEM((devices, 8, 128), jnp.int32),
            pltpu.SMEM((devices, 8, 128), jnp.int32),
            pltpu.VMEM((2, 8, 128), jnp.int32),
            pltpu.SMEM((2, 8, 128), jnp.int32),
            dma((min(3, parts),)),
            dma,
            dma((parts,)),
            dma((2,)),
            dma,
            dma,
            dma,
            dma,
            dma,
            dma,
            dma,
            dma((across, PIECES)),
            dma,
            dma,
            dma,
            dma,
            dma((shares, PIECES)),
            dma,
            dma,
            dma((parts, half)),
            dma,
            dma,
            dma,
            dma((4,)),
        ],
        compiler_params=pltpu.CompilerParams(
            collective_id=1, has_side_effects=True, vmem_limit_bytes=50 * 2**20
        ),
    )(
        slot_order,
        slot_start,
        diffusivity,
        eigen_rates,
        radial_left_factor,
        radial_right,
        coefficients.reshape(parts, rows, rads, packed),
        legendre.reshape(packed, lats),
    )


def dense(
    rads,
    modes,
    arguments,
):
    (
        coefficients,
        legendre,
        radial_left_factor,
        radial_right,
        eigen_rates,
        diffusivity,
        slot_order,
        slot_start,
    ) = arguments
    packed, lats = legendre.shape[2:]
    radii = radial_right.shape[1]
    fields, parts_count = coefficients.shape[:2]
    parts = fields * parts_count
    devices = rads * modes
    rows, columns = radii // rads, lats // modes
    smem = pl.BlockSpec(memory_space=pltpu.SMEM)
    vmem = pl.BlockSpec(memory_space=pltpu.VMEM)
    hbm = pl.BlockSpec(memory_space=pltpu.HBM)
    return pl.pallas_call(
        functools.partial(whole_kernel, rads, modes, parts_count),
        out_shape=pltpu.VMEM((parts * devices, rows, 2, columns), jnp.bfloat16),
        in_specs=[smem, smem, smem, vmem, hbm, hbm, hbm, hbm],
        out_specs=pl.BlockSpec(memory_space=pl.ANY),
        scratch_shapes=[
            pltpu.VMEM(radial_left_factor.shape, jnp.float32),
            pltpu.VMEM(radial_right.shape, jnp.float32),
            pltpu.VMEM((parts, rows, rads, packed), jnp.bfloat16),
            pltpu.VMEM((parts, rads, rows, packed), jnp.bfloat16),
            pltpu.VMEM((parts, rads, rows, packed), jnp.bfloat16),
            pltpu.VMEM((packed, lats), jnp.bfloat16),
            pltpu.VMEM((2 * radii, packed), jnp.bfloat16),
            pltpu.VMEM((parts * devices, rows, 2, columns), jnp.bfloat16),
            pltpu.SemaphoreType.DMA((parts,)),
            pltpu.SemaphoreType.DMA,
            pltpu.SemaphoreType.DMA((parts,)),
            pltpu.SemaphoreType.DMA((2,)),
            pltpu.SemaphoreType.DMA,
            pltpu.SemaphoreType.DMA,
            pltpu.SemaphoreType.DMA,
            pltpu.SemaphoreType.DMA,
        ],
        compiler_params=pltpu.CompilerParams(
            collective_id=0, has_side_effects=True, vmem_limit_bytes=46 * 2**20
        ),
    )(
        slot_order,
        slot_start,
        diffusivity,
        eigen_rates,
        radial_left_factor,
        radial_right,
        coefficients.reshape(parts, rows, rads, packed),
        legendre.reshape(packed, lats),
    )


def on_device(rads, modes, *arguments):
    coefficients, legendre, _, radial_right = arguments[:4]
    packed, lats = legendre.shape[2:]
    rows, columns = radial_right.shape[1] // rads, lats // modes
    fields, parts_count = coefficients.shape[:2]
    parts = fields * parts_count
    half, across = rads // 2, rads // PLANES
    groups = half * modes
    window_blocks = packed // BLOCK // 2
    window_units = window_blocks * BLOCK // UNIT
    block_room = 3 * groups * window_blocks // 4
    unit_room = 21 * groups * window_units // 32
    shares = 2 * modes // PLANES
    fits = (
        rads % PLANES == 0
        and 2 * modes % PLANES == 0
        and parts % max(shares, 1) == 0
        and columns % (BLOCK * across) == 0
        and groups <= rads * (packed // columns)
        and unit_room % PIECES == 0
        and unit_room <= 8 * BLOCK
        and across * unit_room * UNIT * (columns // across) <= 2**22
    )
    if fits:
        landed, flag = factored(rads, modes, unit_room, block_room, arguments)
        landed = lax.switch(
            flag[0, 0], (lambda: landed, lambda: dense(rads, modes, arguments))
        )
    else:
        landed = dense(rads, modes, arguments)
    return landed.reshape(fields, parts_count, rads, modes, rows, 2, columns)


def solution(mesh):
    rads, modes = mesh.shape["rad"], mesh.shape["mode"]
    return jax.shard_map(
        functools.partial(on_device, rads, modes),
        mesh=mesh,
        in_specs=(
            P(None, None, "rad", None, "mode", None),
            P("rad", "mode", None, None),
            P(),
            P(),
            P(),
            P(),
            P("rad", "mode", None),
            P("rad", "mode", None),
        ),
        out_specs=P(None, None, None, None, "rad", None, "mode"),
        check_vma=False,
    )
```
